256 devices in a mesh: dp: 32 (over x, z), expert: 8 (over y, core).
Axes of the slice: x: 4, y: 4, z: 8, core: 2. Of those that a mesh axis runs over, the one named last changes fastest.
Arguments:
- tokens: bfloat16 [4096, 4096], P('dp', 'expert'), may hold values from -6 to 6
- expert_ids: int32 [4096, 8], P('dp'), may hold values from 0 to 31, all different within a row; in each aligned block of 128 rows (0 to 127, 128 to 255, ...) at most 40 rows name the same one
- scores: float32 [4096, 8], P('dp'), may hold values from 0.05 to 1
- weight_in: bfloat16 [32, 4096, 2048], P('dp', 'expert'), may hold values from -0.09375 to 0.09375
- weight_out: bfloat16 [32, 1024, 4096], P('dp', None, 'expert'), may hold values from -0.1875 to 0.1875
- out_grad: bfloat16 [4096, 4096], P('dp', 'expert'), may hold values from -6 to 6
Outputs:
- layer_out: bfloat16 [4096, 4096], P('dp', 'expert')
- tokens_grad: bfloat16 [4096, 4096], P('dp', 'expert')
- scores_grad: float32 [4096, 8], P('dp')
- w_in_grad: bfloat16 [32, 4096, 2048], P('dp', 'expert')
- w_out_grad: bfloat16 [32, 1024, 4096], P('dp', None, 'expert')
The draws below stay inside these ranges and needn't reach their ends.
Inputs may be any that keep to these rules, and one draw needn't show every extreme that they name: `expert_ids`: the 8 experts of a token differ. Among the 128 consecutive tokens of one index of dp no expert is named by more than 40 choices, and in every draw some such block names some expert exactly 40 times.
All inputs are finite; a program needn't handle non-finite values.
Results may differ from the reference program's by a relative error of at most 0.0064.
Values may be sent and summed in bfloat16 or wider, within the bound.
No kernel may reach another device: no remote copies, remote signals or barrier semaphores. Data moves between devices by JAX's collectives and lax.ppermute only.
A program may use at most 128 MiB of HBM per device.

```python
import math
import jax
import jax.numpy as jnp
import numpy as np
from jax import lax

D = 4096
FF = 1024
TOP = 8
TOK_DEV = 128
EXPERTS = 32
CAP = 40
TOKENS = 4096
N_DP = 32


def block_scale(rng, shape, pieces, smallest, largest):
    factor_of = 1.0
    for dim, blocks in pieces:
        draws = jax.random.uniform(jax.random.fold_in(jax.random.fold_in(rng, 6), dim), (blocks,), jnp.float32, smallest / len(pieces), largest / len(pieces))
        factor_of = factor_of * jnp.repeat(jnp.exp(draws), shape[dim] // blocks).reshape((-1,) + (1,) * (len(shape) - 1 - dim))
    return factor_of


def routed_block(key, own, number, rows, count, top, bound, skew):
    ranking = jax.random.permutation(key, count)
    crowded, common = shares(count, rows * top, bound, skew, True), shares(count, rows * top, bound, skew, False)
    places = jnp.arange(count)

    def named(tallies, rotation):
        used = int((tallies > 0).sum())
        fixed = max(1, used // 4)
        moved = fixed + (places - fixed + rotation * (used - fixed)) % max(1, count - fixed)
        return jnp.zeros((count,), jnp.int32).at[ranking[jnp.where(places < fixed, places, moved)]].set(jnp.asarray(tallies, jnp.int32))

    tallies = jnp.where(number % 4 == 0, named(crowded, number // 4), named(common, number - number // 4 - 1))
    mixed = jax.random.permutation(jax.random.fold_in(own, 3), count)
    giver, receiver = mixed[0:count // 2 * 2:2], mixed[1:count // 2 * 2:2]
    slack = jnp.minimum(tallies[giver] - 1, bound - tallies[receiver]) // 2
    slack = jnp.where((giver == ranking[0]) | (receiver == ranking[0]) | (tallies[receiver] == 0), 0, jnp.maximum(slack, 0))
    moved = jax.random.randint(jax.random.fold_in(own, 4), (count // 2,), 0, 1 << 20) % (slack + 1)
    tallies = tallies.at[giver].add(-moved).at[receiver].add(moved)
    items = jnp.searchsorted(jnp.cumsum(tallies), jnp.arange(rows * top), side="right").astype(jnp.int32)
    listing = items.reshape(top, rows).T
    listing = listing[jax.random.permutation(jax.random.fold_in(own, 1), rows)]
    rotation = jax.random.randint(jax.random.fold_in(own, 2), (rows, 1), 0, top)
    return jnp.take_along_axis(listing, (jnp.arange(top)[None, :] + rotation) % top, axis=1)


def shares(number_of, total, most, lean, full):
    weights = [(1 << 20) // math.isqrt(standing ** lean) + 1 for standing in range(1, number_of + 1)]
    largest = most if full else min(most, max(-(-total // number_of), total * weights[0] // sum(weights)))
    least = 1 if total - largest >= number_of - 1 else 0
    given, rest = [largest] + [least] * (number_of - 1), total - largest - least * (number_of - 1)
    while rest > 0:
        movable = [i for i in range(1, number_of) if given[i] < largest] or [i for i in range(1, number_of) if given[i] < most]
        mass, left = sum([weights[i] for i in movable]), rest
        for i in movable:
            more = min(most - given[i], max(1, left * weights[i] // mass), rest)
            given[i] = given[i] + more
            rest = rest - more
    return np.array(given)


def noise(stream_key, dims, deviation, bound, split=(), kind=jnp.bfloat16):
    values = deviation * jax.random.normal(stream_key, dims, jnp.float32)
    if split:
        values = values * block_scale(stream_key, dims, split, -0.22, 0.18)
    return jnp.clip(values, -bound, bound).astype(kind)


def setup_inputs(seed: int = 0) -> dict:
    seeds = jax.random.split(jax.random.key(seed), 7)
    tokens = noise(seeds[0], (TOKENS, D), 1.0, 6.0, ((0, 32), (1, 8)))
    expert_ids_keys = jax.random.split(jax.random.fold_in(seeds[1], 1), TOKENS // TOK_DEV)
    expert_ids_turns = jax.random.permutation(jax.random.fold_in(seeds[1], 3), TOKENS // TOK_DEV)
    expert_ids = jax.vmap(lambda own, number: routed_block(jax.random.fold_in(seeds[1], 2), own, number, TOK_DEV, EXPERTS, TOP, CAP, 2))(expert_ids_keys, expert_ids_turns).reshape((TOKENS, TOP))
    scores = jnp.clip(jnp.exp(math.log(1.0) - 2.9957323 * jax.random.uniform(seeds[2], (TOKENS, TOP), jnp.float32) ** block_scale(seeds[2], (TOKENS, TOP), ((0, 32),), -0.2, 0.2)), 0.05, 1.0)
    weight_in = noise(seeds[3], (EXPERTS, D, 2 * FF), D ** -0.5, 0.09375, ((0, 32), (1, 8)))
    weight_out = noise(seeds[4], (EXPERTS, FF, D), FF ** -0.5, 0.1875, ((0, 32), (2, 8)))
    out_grad = noise(seeds[5], (TOKENS, D), 1.0, 6.0, ((0, 32), (1, 8)))
    return {"tokens": tokens, "expert_ids": expert_ids, "scores": scores, "weight_in": weight_in, "weight_out": weight_out, "out_grad": out_grad}


ROUTE_SCALE = 2.5


def expert_pass(weight_in_e, weight_out_e, rows_x, rows_grad):
    gate_up = jnp.dot(rows_x, weight_in_e, preferred_element_type=jnp.float32)
    gate = gate_up[:, :FF]
    upward = gate_up[:, FF:]
    sigma = jax.nn.sigmoid(gate)
    hidden = (gate * sigma * upward).astype(jnp.bfloat16)
    expert_out = jnp.dot(hidden, weight_out_e, preferred_element_type=jnp.float32).astype(jnp.bfloat16)
    hidden_grad = jnp.dot(rows_grad, weight_out_e.T, preferred_element_type=jnp.float32)
    gate_up_grad = jnp.concatenate(
        [hidden_grad * upward * sigma * (1.0 + gate * (1.0 - sigma)), hidden_grad * gate * sigma], axis=1
    ).astype(jnp.bfloat16)
    choice_grad = jnp.dot(gate_up_grad, weight_in_e.T, preferred_element_type=jnp.float32).astype(jnp.bfloat16)
    in_weight = jnp.dot(rows_x.T, gate_up_grad, preferred_element_type=jnp.float32).astype(jnp.bfloat16)
    out_weight = jnp.dot(hidden.T, rows_grad, preferred_element_type=jnp.float32).astype(jnp.bfloat16)
    return expert_out, choice_grad, in_weight, out_weight


def reference(tokens, expert_ids, scores, weight_in, weight_out, out_grad):
    blocks = N_DP
    per_block = TOK_DEV * TOP
    routed_all = blocks * per_block
    ids_blocks = expert_ids.reshape(blocks, per_block)
    expert_hot = (ids_blocks[:, :, None] == jnp.arange(EXPERTS, dtype=jnp.int32)[None, None, :]).astype(jnp.int32)
    earlier = jnp.sum((jnp.cumsum(expert_hot, axis=1) - expert_hot) * expert_hot, axis=2)
    position = jnp.arange(blocks, dtype=jnp.int32)[:, None] * CAP + earlier
    routed_index = jnp.arange(routed_all, dtype=jnp.int32).reshape(blocks, per_block)
    table = jnp.full((EXPERTS, blocks * CAP), routed_all, jnp.int32).at[ids_blocks, position].set(routed_index)

    score_total = jnp.sum(scores, axis=1, keepdims=True)
    route_weights = ROUTE_SCALE * scores / score_total
    tokens_pad = jnp.concatenate([tokens, jnp.zeros((1, D), tokens.dtype)], axis=0)
    grad_pad = jnp.concatenate([out_grad.astype(jnp.float32), jnp.zeros((1, D), jnp.float32)], axis=0)
    weight_flat = jnp.concatenate([route_weights.reshape(-1), jnp.zeros((1,), jnp.float32)], axis=0)

    def one_expert(operands):
        weight_in_e, weight_out_e, entries = operands
        owner = entries // TOP
        rows_x = tokens_pad[owner]
        rows_grad = (weight_flat[entries][:, None] * grad_pad[owner]).astype(jnp.bfloat16)
        return expert_pass(weight_in_e, weight_out_e, rows_x, rows_grad)

    expert_out, choice_grad, w_in_grad, w_out_grad = lax.map(one_expert, (weight_in, weight_out, table))
    flat_table = table.reshape(-1)
    out_rows = jnp.zeros((routed_all + 1, D), expert_out.dtype).at[flat_table].set(expert_out.reshape(-1, D))
    grad_rows = jnp.zeros((routed_all + 1, D), choice_grad.dtype).at[flat_table].set(choice_grad.reshape(-1, D))
    picked = out_rows[:routed_all].astype(jnp.float32).reshape(TOKENS, TOP, D)
    layer_out = jnp.sum(route_weights[:, :, None] * picked, axis=1).astype(jnp.bfloat16)
    tokens_grad = jnp.sum(grad_rows[:routed_all].astype(jnp.float32).reshape(TOKENS, TOP, D), axis=1).astype(jnp.bfloat16)
    choice_dot = jnp.sum(out_grad.astype(jnp.float32)[:, None, :] * picked, axis=2)
    scores_grad = (ROUTE_SCALE * choice_dot - jnp.sum(choice_dot * route_weights, axis=1, keepdims=True)) / score_total
    return layer_out, tokens_grad, scores_grad, w_in_grad, w_out_grad
```

```python
import jax
import jax.numpy as jnp
from jax import lax
from jax.sharding import PartitionSpec as P

ROUTE_SCALE = 2.5
BF = jnp.bfloat16
F32 = jnp.float32


def permute_y(v, step, n_y):
    return lax.ppermute(
        v, "expert", [(2 * y + c, 2 * ((y + step) % n_y) + c) for y in range(n_y) for c in range(2)]
    )


def permute_core(v, n_y):
    return lax.ppermute(
        v, "expert", [(2 * y + c, 2 * y + 1 - c) for y in range(n_y) for c in range(2)]
    )


def dot(a, b):
    return jnp.dot(a, b, preferred_element_type=F32)


def dot_t(a, b):
    return jnp.einsum("rd,fd->rf", a, b, preferred_element_type=F32)


def gather_dot(a, b):
    return jnp.einsum("rd,rf->df", a, b, preferred_element_type=F32)


def reduce_rows(own, other, n_y):
    rows = own.shape[0] // n_y
    half = rows // 2
    got = permute_core(other.astype(BF), n_y)
    total = own + got.astype(F32)
    b0, b1, b2, b3 = (total[i * rows : (i + 1) * rows] for i in range(4))
    up2 = permute_y(b2[:half].astype(BF), 1, n_y)
    dn2 = permute_y(b2[half:].astype(BF), -1, n_y)
    up1b = permute_y(b1[half:].astype(BF), 1, n_y)
    dn1a = permute_y(b3[:half].astype(BF), -1, n_y)
    up1a = permute_y((b1[:half] + up2.astype(F32)).astype(BF), 1, n_y)
    dn1b = permute_y((b3[half:] + dn2.astype(F32)).astype(BF), -1, n_y)
    first = b0[:half] + dn1a.astype(F32) + up1a.astype(F32)
    second = b0[half:] + up1b.astype(F32) + dn1b.astype(F32)
    return jnp.concatenate([first, second], axis=0)


def gather_rows(v, n_y):
    half = v.shape[0] // 2
    a, b = v[:half], v[half:]
    from_dn_a = permute_y(a, 1, n_y)
    from_up_b = permute_y(b, -1, n_y)
    from_dn_b = permute_y(b, 1, n_y)
    from_up_a = permute_y(a, -1, n_y)
    far_a = permute_y(from_dn_a, 1, n_y)
    far_b = permute_y(from_up_b, -1, n_y)
    own = jnp.concatenate([a, b, from_up_a, from_up_b, far_a, far_b, from_dn_a, from_dn_b], axis=0)
    other = permute_core(own, n_y)
    return own, other


def relative(slab, y, core, n_y):
    rows = slab.shape[0] // (2 * n_y)

    def block(c, d):
        return lax.dynamic_slice_in_dim(slab, (c * n_y + (y + d) % n_y) * rows, rows, 0)

    own = jnp.concatenate([block(core, d) for d in range(n_y)], axis=0)
    other = jnp.concatenate([block(1 - core, d) for d in range(n_y)], axis=0)
    return own, other


def absolute(own, other, y, core, n_y):
    rows = own.shape[0] // n_y
    both = jnp.concatenate([own, other], axis=0)
    blocks = []
    for c in range(2):
        for yy in range(n_y):
            place = jnp.where(core == c, 0, n_y) + (yy - y) % n_y
            blocks.append(lax.dynamic_slice_in_dim(both, place * rows, rows, 0))
    return jnp.concatenate(blocks, axis=0)


def body(tokens, expert_ids, scores, weight_in, weight_out, out_grad):
    n_data = lax.axis_size("dp")
    n_y = lax.axis_size("expert") // 2
    here = lax.axis_index("expert")
    y, core = here // 2, here % 2
    tok_count, width = tokens.shape
    top_count = expert_ids.shape[1]
    hidden_units = weight_out.shape[1]
    capacity = min(tok_count, 5 * tok_count * top_count // (4 * n_data))
    slots = n_data * capacity

    ids_t = expert_ids.T
    scores_t = scores.T
    score_total = jnp.sum(scores_t, axis=0, keepdims=True)
    weights_t = ROUTE_SCALE * scores_t / score_total
    named = ids_t[:, None, :] == jnp.arange(n_data, dtype=jnp.int32)[None, :, None]
    hot = jnp.sum(named.astype(F32), axis=0)
    weight_of = jnp.sum(jnp.where(named, weights_t[:, None, :], 0.0), axis=0)
    before = (
        jnp.arange(tok_count, dtype=jnp.int32)[:, None] < jnp.arange(tok_count, dtype=jnp.int32)[None, :]
    ).astype(BF)
    rank = dot(hot.astype(BF), before)
    position = jnp.where(hot > 0.0, rank, -1.0).astype(jnp.int32)
    placed = position[:, None, :] == jnp.arange(capacity, dtype=jnp.int32)[None, :, None]
    place = placed.astype(BF).reshape(slots, tok_count)
    weight_place = jnp.where(placed, weight_of[:, None, :], 0.0).reshape(slots, tok_count)
    row_weight = jnp.sum(weight_place, axis=1, keepdims=True)

    token_send = dot(place, tokens).astype(BF)
    grad_rows = dot(place, out_grad)
    grad_send = (row_weight * grad_rows).astype(BF)
    grad_rows = grad_rows.astype(BF)

    def exchange(v):
        v = v.reshape(n_data, capacity, width)
        return lax.all_to_all(v, "dp", split_axis=0, concat_axis=0, tiled=True).reshape(slots, width)

    in_slab, out_slab = weight_in[0], weight_out[0]
    token_slab = exchange(token_send)
    token_slab, grad_send = lax.optimization_barrier((token_slab, grad_send))
    grad_slab = exchange(grad_send)

    tok_own, tok_other = relative(token_slab, y, core, n_y)
    gate_up = reduce_rows(dot(tok_own, in_slab), dot(tok_other, in_slab), n_y)
    gate, up = gate_up[:, :hidden_units], gate_up[:, hidden_units:]
    sig = jax.nn.sigmoid(gate)
    hidden = (gate * sig * up).astype(BF)
    hid_own, hid_other = gather_rows(hidden, n_y)

    grad_own, grad_other = relative(grad_slab, y, core, n_y)
    hidden_grad = reduce_rows(dot_t(grad_own, out_slab), dot_t(grad_other, out_slab), n_y)
    gate_up_grad = jnp.concatenate(
        [hidden_grad * up * sig * (1.0 + gate * (1.0 - sig)), hidden_grad * gate * sig], axis=1
    ).astype(BF)

    expert_out = absolute(
        dot(hid_own, out_slab).astype(BF), dot(hid_other, out_slab).astype(BF), y, core, n_y
    )
    out_back = exchange(expert_out)

    gug_own, gug_other = gather_rows(gate_up_grad, n_y)
    choice_grad = absolute(
        dot_t(gug_own, in_slab).astype(BF), dot_t(gug_other, in_slab).astype(BF), y, core, n_y
    )
    grad_back = exchange(choice_grad)

    w_out_grad = (gather_dot(hid_own, grad_own) + gather_dot(hid_other, grad_other)).astype(BF)
    w_in_grad = (gather_dot(tok_own, gug_own) + gather_dot(tok_other, gug_other)).astype(BF)

    high = lax.reduce_precision(weight_place, 8, 7)
    low = (weight_place - high).astype(BF)
    high = high.astype(BF)
    layer_out = (gather_dot(high, out_back) + gather_dot(low, out_back)).astype(BF)
    slot_dot = jnp.sum(grad_rows.astype(F32) * out_back.astype(F32), axis=1)
    slot_dot = lax.psum(slot_dot.reshape(n_data, capacity), "expert")
    dot_of = jnp.sum(jnp.where(placed, slot_dot[:, :, None], 0.0), axis=1)
    choice_dot = jnp.sum(jnp.where(named, dot_of[None, :, :], 0.0), axis=1)
    scores_grad = (
        ROUTE_SCALE * choice_dot - jnp.sum(choice_dot * weights_t, axis=0, keepdims=True)
    ) / score_total
    tokens_grad = gather_dot(place, grad_back).astype(BF)
    return layer_out, tokens_grad, scores_grad.T, w_in_grad[None], w_out_grad[None]


def solution(mesh):
    return jax.shard_map(
        body,
        mesh=mesh,
        in_specs=(
            P("dp", "expert"),
            P("dp", None),
            P("dp", None),
            P("dp", "expert", None),
            P("dp", None, "expert"),
            P("dp", "expert"),
        ),
        out_specs=(
            P("dp", "expert"),
            P("dp", "expert"),
            P("dp", None),
            P("dp", "expert", None),
            P("dp", None, "expert"),
        ),
        check_vma=False,
    )
```

```python
import jax
import jax.numpy as jnp
from jax import lax
from jax.sharding import PartitionSpec as P


ROUTE_SCALE = 2.5
BF = jnp.bfloat16
F32 = jnp.float32


def permute_y(v, step, n_y):
    return lax.ppermute(
        v, "expert", [(2 * y + c, 2 * ((y + step) % n_y) + c) for y in range(n_y) for c in range(2)]
    )


def permute_core(v, n_y):
    return lax.ppermute(
        v, "expert", [(2 * y + c, 2 * y + 1 - c) for y in range(n_y) for c in range(2)]
    )


def dot(a, b):
    return jnp.dot(a, b, preferred_element_type=F32)


def dot_t(a, b):
    return jnp.einsum("rd,fd->rf", a, b, preferred_element_type=F32)


def gather_dot(a, b):
    return jnp.einsum("rd,rf->df", a, b, preferred_element_type=F32)


def reduce_rows(product, own, part, w_own, w_part, n_y):
    rows = own.shape[0] // n_y
    far = (product(own[rows:], w_own) + product(part[rows:], w_part)).astype(BF)
    got = [
        permute_y(far[(d - 1) * rows : d * rows], d, n_y).astype(F32) for d in range(1, n_y)
    ]
    total = product(own[:rows], w_own) + product(part[:rows], w_part)
    for piece in got:
        total = total + piece
    return total


def gather_rows(v, n_y):
    return jnp.concatenate([v] + [permute_y(v, -d, n_y) for d in range(1, n_y)], axis=0)


def relative(slab, half, y, n_y):
    rows = slab.shape[0] // (2 * n_y)
    return jnp.concatenate(
        [
            lax.dynamic_slice_in_dim(slab, (half * n_y + (y + d) % n_y) * rows, rows, 0)
            for d in range(n_y)
        ],
        axis=0,
    )


def absolute(part, y, n_y):
    rows = part.shape[0] // n_y
    return jnp.concatenate(
        [lax.dynamic_slice_in_dim(part, ((yy - y) % n_y) * rows, rows, 0) for yy in range(n_y)],
        axis=0,
    )


def both_halves(own, other, core):
    flat = jnp.where(core == 0, jnp.stack([own, other]), jnp.stack([other, own]))
    return flat.reshape(2 * own.shape[0], own.shape[1])


def body(tokens, expert_ids, scores, weight_in, weight_out, out_grad):
    n_data = lax.axis_size("dp")
    n_y = lax.axis_size("expert") // 2
    here = lax.axis_index("expert")
    y, core = lax.div(here, 2), lax.rem(here, 2)
    tok_count, width = tokens.shape
    top_count = expert_ids.shape[1]
    hidden_units = weight_out.shape[1]
    capacity = min(tok_count, 5 * tok_count * top_count // (4 * n_data))
    slots = n_data * capacity

    ids_t = expert_ids.T
    scores_t = scores.T
    score_total = jnp.sum(scores_t, axis=0, keepdims=True)
    weights_t = ROUTE_SCALE * scores_t / score_total
    named = ids_t[:, None, :] == jnp.arange(n_data, dtype=jnp.int32)[None, :, None]
    hot = jnp.sum(named.astype(F32), axis=0)
    weight_of = jnp.sum(jnp.where(named, weights_t[:, None, :], 0.0), axis=0)
    before = (
        jnp.arange(tok_count, dtype=jnp.int32)[:, None] < jnp.arange(tok_count, dtype=jnp.int32)[None, :]
    ).astype(BF)
    rank = dot(hot.astype(BF), before)
    position = jnp.where(hot > 0.0, rank, -1.0).astype(jnp.int32)
    placed = position[:, None, :] == jnp.arange(capacity, dtype=jnp.int32)[None, :, None]
    place = placed.astype(BF).reshape(slots, tok_count)

    token_send = dot(place, tokens).astype(BF)

    def exchange(v):
        v = v.reshape(n_data, capacity, width)
        return lax.all_to_all(v, "dp", split_axis=0, concat_axis=0, tiled=True).reshape(slots, width)

    in_own, out_own = weight_in[0], weight_out[0]
    token_slab = exchange(token_send)
    in_part = permute_core(in_own, n_y)
    out_part = permute_core(out_own, n_y)

    weight_place = jnp.where(placed, weight_of[:, None, :], 0.0).reshape(slots, tok_count)
    row_weight = jnp.sum(weight_place, axis=1, keepdims=True)
    grad_rows = dot(place, out_grad)
    grad_send = (row_weight * grad_rows).astype(BF)
    grad_rows = grad_rows.astype(BF)
    token_slab, grad_send, in_part, out_part = lax.optimization_barrier(
        (token_slab, grad_send, in_part, out_part)
    )
    grad_slab = exchange(grad_send)

    tok_part = permute_core(relative(token_slab, 1 - core, y, n_y), n_y)
    tok_own = relative(token_slab, core, y, n_y)
    gate_up = reduce_rows(dot, tok_own, tok_part, in_own, in_part, n_y)
    gate, up = gate_up[:, :hidden_units], gate_up[:, hidden_units:]
    sig = jax.nn.sigmoid(gate)
    hidden = (gate * sig * up).astype(BF)
    hid = gather_rows(hidden, n_y)

    grad_slab, _ = lax.optimization_barrier((grad_slab, hidden))
    grad_part = permute_core(relative(grad_slab, 1 - core, y, n_y), n_y)
    grad_own = relative(grad_slab, core, y, n_y)
    hidden_grad = reduce_rows(dot_t, grad_own, grad_part, out_own, out_part, n_y)
    gate_up_grad = jnp.concatenate(
        [hidden_grad * up * sig * (1.0 + gate * (1.0 - sig)), hidden_grad * gate * sig], axis=1
    ).astype(BF)

    out_other = permute_core(absolute(dot(hid, out_part).astype(BF), y, n_y), n_y)
    out_mine = absolute(dot(hid, out_own).astype(BF), y, n_y)
    expert_out = both_halves(out_mine, out_other, core)
    out_back = exchange(expert_out)

    gug = gather_rows(gate_up_grad, n_y)
    grad_other = permute_core(absolute(dot_t(gug, in_part).astype(BF), y, n_y), n_y)
    grad_mine = absolute(dot_t(gug, in_own).astype(BF), y, n_y)
    choice_grad = both_halves(grad_mine, grad_other, core)
    out_back, choice_grad = lax.optimization_barrier((out_back, choice_grad))
    grad_back = exchange(choice_grad)

    tok_part, tok_own, _ = lax.optimization_barrier((tok_part, tok_own, choice_grad))
    w_out_other = permute_core(gather_dot(hid, grad_part), n_y)
    w_out_grad = (gather_dot(hid, grad_own) + w_out_other).astype(BF)
    w_in_other = permute_core(gather_dot(tok_part, gug), n_y)
    w_in_grad = (gather_dot(tok_own, gug) + w_in_other).astype(BF)

    high = lax.reduce_precision(weight_place, 8, 7)
    low = (weight_place - high).astype(BF)
    high = high.astype(BF)
    layer_out = (gather_dot(high, out_back) + gather_dot(low, out_back)).astype(BF)
    slot_dot = jnp.sum(grad_rows.astype(F32) * out_back.astype(F32), axis=1)
    slot_dot = lax.psum(slot_dot.reshape(n_data, capacity), "expert")
    dot_of = jnp.sum(jnp.where(placed, slot_dot[:, :, None], 0.0), axis=1)
    choice_dot = jnp.sum(jnp.where(named, dot_of[None, :, :], 0.0), axis=1)
    scores_grad = (
        ROUTE_SCALE * choice_dot - jnp.sum(choice_dot * weights_t, axis=0, keepdims=True)
    ) / score_total
    tokens_grad = gather_dot(place, grad_back).astype(BF)
    return layer_out, tokens_grad, scores_grad.T, w_in_grad[None], w_out_grad[None]


def solution(mesh):
    return jax.shard_map(
        body,
        mesh=mesh,
        in_specs=(
            P("dp", "expert"),
            P("dp", None),
            P("dp", None),
            P("dp", "expert", None),
            P("dp", None, "expert"),
            P("dp", "expert"),
        ),
        out_specs=(
            P("dp", "expert"),
            P("dp", "expert"),
            P("dp", None),
            P("dp", "expert", None),
            P("dp", None, "expert"),
        ),
        check_vma=False,
    )
```

```python
import jax
import jax.numpy as jnp
from jax import lax
from jax.sharding import PartitionSpec as P


ROUTE_SCALE = 2.5
BF = jnp.bfloat16
F32 = jnp.float32


def permute_y(v, step, n_y):
    return lax.ppermute(
        v, "expert", [(2 * y + c, 2 * ((y + step) % n_y) + c) for y in range(n_y) for c in range(2)]
    )


def permute_core(v, n_y):
    return lax.ppermute(
        v, "expert", [(2 * y + c, 2 * y + 1 - c) for y in range(n_y) for c in range(2)]
    )


def dot(a, b):
    return jnp.dot(a, b, preferred_element_type=F32)


def dot_t(a, b):
    return jnp.einsum("rd,fd->rf", a, b, preferred_element_type=F32)


def gather_dot(a, b):
    return jnp.einsum("rd,rf->df", a, b, preferred_element_type=F32)


def permute_xor(v, bit, n_y):
    return lax.ppermute(v, "expert", [(e, e ^ bit) for e in range(2 * n_y)])


def reduce_rows(product, own, part, w_own, w_part, n_y):
    rows = own.shape[0] // n_y
    far = (product(own[rows:], w_own) + product(part[rows:], w_part)).astype(BF)
    got = [
        permute_y(far[(d - 1) * rows : d * rows], d, n_y).astype(F32) for d in range(1, n_y)
    ]
    total = product(own[:rows], w_own) + product(part[:rows], w_part)
    for piece in got:
        total = total + piece
    return total


def gather_rows(v, n_y):
    return jnp.concatenate([v] + [permute_y(v, -d, n_y) for d in range(1, n_y)], axis=0)


def relative(slab, half, y, n_y):
    rows = slab.shape[0] // (2 * n_y)
    return jnp.concatenate(
        [
            lax.dynamic_slice_in_dim(slab, (half * n_y + (y + d) % n_y) * rows, rows, 0)
            for d in range(n_y)
        ],
        axis=0,
    )


def absolute(part, y, n_y):
    rows = part.shape[0] // n_y
    return jnp.concatenate(
        [lax.dynamic_slice_in_dim(part, ((yy - y) % n_y) * rows, rows, 0) for yy in range(n_y)],
        axis=0,
    )


def both_halves(own, other, core):
    flat = jnp.where(core == 0, jnp.stack([own, other]), jnp.stack([other, own]))
    return flat.reshape(2 * own.shape[0], own.shape[1])


def body(tokens, expert_ids, scores, weight_in, weight_out, out_grad):
    n_data = lax.axis_size("dp")
    n_y = lax.axis_size("expert") // 2
    here = lax.axis_index("expert")
    y, core = lax.div(here, 2), lax.rem(here, 2)
    tok_count, width = tokens.shape
    top_count = expert_ids.shape[1]
    hidden_units = weight_out.shape[1]
    capacity = min(tok_count, 5 * tok_count * top_count // (4 * n_data))
    slots = n_data * capacity

    ids_t = expert_ids.T
    scores_t = scores.T
    named = ids_t[:, None, :] == jnp.arange(n_data, dtype=jnp.int32)[None, :, None]
    hot = jnp.sum(named.astype(F32), axis=0)
    before = (
        jnp.arange(tok_count, dtype=jnp.int32)[:, None] < jnp.arange(tok_count, dtype=jnp.int32)[None, :]
    ).astype(BF)
    rank = dot(hot.astype(BF), before)
    position = jnp.where(hot > 0.0, rank, -1.0).astype(jnp.int32)
    placed = position[:, None, :] == jnp.arange(capacity, dtype=jnp.int32)[None, :, None]
    place = placed.astype(BF).reshape(slots, tok_count)

    token_send = dot(place, tokens).astype(BF)

    def exchange(v):
        v = v.reshape(n_data, capacity, width)
        return lax.all_to_all(v, "dp", split_axis=0, concat_axis=0, tiled=True).reshape(slots, width)

    in_own, out_own = weight_in[0], weight_out[0]
    token_slab = exchange(token_send)
    in_part = permute_core(in_own, n_y)
    out_part = permute_core(out_own, n_y)

    score_total = jnp.sum(scores_t, axis=0, keepdims=True)
    weights_t = ROUTE_SCALE * scores_t / score_total
    weight_of = jnp.sum(jnp.where(named, weights_t[:, None, :], 0.0), axis=0)
    weight_place = jnp.where(placed, weight_of[:, None, :], 0.0).reshape(slots, tok_count)
    row_weight = jnp.sum(weight_place, axis=1, keepdims=True)
    grad_rows = dot(place, out_grad)
    grad_send = (row_weight * grad_rows).astype(BF)
    grad_send, grad_rows = lax.optimization_barrier((grad_send, grad_rows.astype(BF)))
    grad_slab = exchange(grad_send)

    tok_part = permute_core(relative(token_slab, 1 - core, y, n_y), n_y)
    tok_own = relative(token_slab, core, y, n_y)
    gate_up = reduce_rows(dot, tok_own, tok_part, in_own, in_part, n_y)
    gate, up = gate_up[:, :hidden_units], gate_up[:, hidden_units:]
    sig = jax.nn.sigmoid(gate)
    hidden = (gate * sig * up).astype(BF)
    hid = gather_rows(hidden, n_y)

    grad_slab, _ = lax.optimization_barrier((grad_slab, hidden))
    grad_part = permute_core(relative(grad_slab, 1 - core, y, n_y), n_y)
    grad_own = relative(grad_slab, core, y, n_y)
    hidden_grad = reduce_rows(dot_t, grad_own, grad_part, out_own, out_part, n_y)
    gate_up_grad = jnp.concatenate(
        [hidden_grad * up * sig * (1.0 + gate * (1.0 - sig)), hidden_grad * gate * sig], axis=1
    ).astype(BF)

    out_other = permute_core(absolute(dot(hid, out_part).astype(BF), y, n_y), n_y)
    out_mine = absolute(dot(hid, out_own).astype(BF), y, n_y)
    expert_out = both_halves(out_mine, out_other, core)
    out_back = exchange(expert_out)

    gug = gather_rows(gate_up_grad, n_y)
    grad_other = permute_core(absolute(dot_t(gug, in_part).astype(BF), y, n_y), n_y)
    grad_mine = absolute(dot_t(gug, in_own).astype(BF), y, n_y)
    choice_grad = both_halves(grad_mine, grad_other, core)
    grad_back = exchange(choice_grad)

    tok_part, tok_own, _ = lax.optimization_barrier((tok_part, tok_own, choice_grad))
    w_out_other = permute_core(gather_dot(hid, grad_part), n_y)
    w_out_grad = (gather_dot(hid, grad_own) + w_out_other).astype(BF)
    w_in_other = permute_core(gather_dot(tok_part, gug), n_y)
    w_in_grad = (gather_dot(tok_own, gug) + w_in_other).astype(BF)

    high = lax.reduce_precision(weight_place, 8, 7)
    low = (weight_place - high).astype(BF)
    high = high.astype(BF)
    layer_out = (gather_dot(high, out_back) + gather_dot(low, out_back)).astype(BF)
    slot_dot = jnp.sum(grad_rows.astype(F32) * out_back.astype(F32), axis=1)
    slot_dot = slot_dot.reshape(n_data, capacity)
    bit = 1
    while bit < 2 * n_y:
        slot_dot = slot_dot + permute_xor(slot_dot, bit, n_y)
        bit = 2 * bit
    dot_of = jnp.sum(jnp.where(placed, slot_dot[:, :, None], 0.0), axis=1)
    choice_dot = jnp.sum(jnp.where(named, dot_of[None, :, :], 0.0), axis=1)
    scores_grad = (
        ROUTE_SCALE * choice_dot - jnp.sum(choice_dot * weights_t, axis=0, keepdims=True)
    ) / score_total
    tokens_grad = gather_dot(place, grad_back).astype(BF)
    return layer_out, tokens_grad, scores_grad.T, w_in_grad[None], w_out_grad[None]


def solution(mesh):
    return jax.shard_map(
        body,
        mesh=mesh,
        in_specs=(
            P("dp", "expert"),
            P("dp", None),
            P("dp", None),
            P("dp", "expert", None),
            P("dp", None, "expert"),
            P("dp", "expert"),
        ),
        out_specs=(
            P("dp", "expert"),
            P("dp", "expert"),
            P("dp", None),
            P("dp", "expert", None),
            P("dp", None, "expert"),
        ),
        check_vma=False,
    )
```

```python
import jax
import jax.numpy as jnp
from jax import lax
from jax.experimental import pallas as pl
from jax.sharding import PartitionSpec as P


ROUTE_SCALE = 2.5
BF = jnp.bfloat16
F32 = jnp.float32


def permute_y(v, step, n_y):
    return lax.ppermute(
        v, "expert", [(2 * y + c, 2 * ((y + step) % n_y) + c) for y in range(n_y) for c in range(2)]
    )


def permute_core(v, n_y):
    return lax.ppermute(
        v, "expert", [(2 * y + c, 2 * y + 1 - c) for y in range(n_y) for c in range(2)]
    )


def dot(a, b):
    return jnp.dot(a, b, preferred_element_type=F32)


def dot_t(a, b):
    return jnp.einsum("rd,fd->rf", a, b, preferred_element_type=F32)


def gather_dot(a, b):
    return jnp.einsum("rd,rf->df", a, b, preferred_element_type=F32)


def permute_xor(v, bit, n_y):
    return lax.ppermute(v, "expert", [(e, e ^ bit) for e in range(2 * n_y)])


def reduce_rows(product, own, part, w_own, w_part, n_y):
    rows = own.shape[0] // n_y
    half = rows // 2
    far = product(own[rows:], w_own) + product(part[rows:], w_part)
    b1, b2, b3 = far[:rows], far[rows : 2 * rows], far[2 * rows :]
    up2 = permute_y(b2[:half].astype(BF), 1, n_y)
    dn2 = permute_y(b2[half:].astype(BF), -1, n_y)
    up1 = jnp.concatenate([b1[:half] + up2.astype(F32), b1[half:]], axis=0).astype(BF)
    dn1 = jnp.concatenate([b3[:half], b3[half:] + dn2.astype(F32)], axis=0).astype(BF)
    got = [permute_y(up1, 1, n_y), permute_y(dn1, -1, n_y)]
    return product(own[:rows], w_own) + product(part[:rows], w_part), got, (up1, dn1)


def add_all(near, got):
    for piece in got:
        near = near + piece.astype(F32)
    return near


def gate_grad_kernel(near, up, dn, factor, out):
    width = near.shape[1]
    grad = near[...] + up[...].astype(F32) + dn[...].astype(F32)
    out[:, :width] = (grad * factor[:, :width]).astype(BF)
    out[:, width:] = (grad * factor[:, width:]).astype(BF)


def gate_grad(near, up, dn, factor):
    rows, width = near.shape
    tile = rows // 2
    narrow = pl.BlockSpec((tile, width), lambda i: (i, 0))
    wide = pl.BlockSpec((tile, 2 * width), lambda i: (i, 0))
    return pl.pallas_call(
        gate_grad_kernel,
        grid=(2,),
        in_specs=[narrow, narrow, narrow, wide],
        out_specs=wide,
        out_shape=jax.ShapeDtypeStruct((rows, 2 * width), BF),
    )(near, up, dn, factor)


def gather_rows(v, n_y):
    half = v.shape[0] // 2
    dn = permute_y(v, 1, n_y)
    up = permute_y(v, -1, n_y)
    far_a = permute_y(dn[:half], 1, n_y)
    far_b = permute_y(up[half:], -1, n_y)
    return jnp.concatenate([v, up, far_a, far_b, dn], axis=0)


def relative(slab, half, y, n_y):
    rows = slab.shape[0] // (2 * n_y)
    return jnp.concatenate(
        [
            lax.dynamic_slice_in_dim(slab, (half * n_y + (y + d) % n_y) * rows, rows, 0)
            for d in range(n_y)
        ],
        axis=0,
    )


def absolute(part, y, n_y):
    rows = part.shape[0] // n_y
    return jnp.concatenate(
        [lax.dynamic_slice_in_dim(part, ((yy - y) % n_y) * rows, rows, 0) for yy in range(n_y)],
        axis=0,
    )


def both_halves(own, other, core):
    flat = jnp.where(core == 0, jnp.stack([own, other]), jnp.stack([other, own]))
    return flat.reshape(2 * own.shape[0], own.shape[1])


def body(tokens, expert_ids, scores, weight_in, weight_out, out_grad):
    n_data = lax.axis_size("dp")
    n_y = lax.axis_size("expert") // 2
    here = lax.axis_index("expert")
    y, core = lax.div(here, 2), lax.rem(here, 2)
    tok_count, width = tokens.shape
    top_count = expert_ids.shape[1]
    hidden_units = weight_out.shape[1]
    capacity = min(tok_count, 5 * tok_count * top_count // (4 * n_data))
    slots = n_data * capacity

    ids_t = expert_ids.T
    scores_t = scores.T
    named = ids_t[:, None, :] == jnp.arange(n_data, dtype=jnp.int32)[None, :, None]
    hot = jnp.sum(named.astype(F32), axis=0)
    before = (
        jnp.arange(tok_count, dtype=jnp.int32)[:, None] < jnp.arange(tok_count, dtype=jnp.int32)[None, :]
    ).astype(BF)
    rank = dot(hot.astype(BF), before)
    position = jnp.where(hot > 0.0, rank, -1.0).astype(jnp.int32)
    placed = position[:, None, :] == jnp.arange(capacity, dtype=jnp.int32)[None, :, None]
    place = placed.astype(BF).reshape(slots, tok_count)

    token_send = dot(place, tokens).astype(BF)

    def exchange(v):
        v = v.reshape(n_data, capacity, width)
        return lax.all_to_all(v, "dp", split_axis=0, concat_axis=0, tiled=True).reshape(slots, width)

    in_own, out_own = weight_in[0], weight_out[0]
    token_slab = exchange(token_send)
    in_part = permute_core(in_own, n_y)
    out_part = permute_core(out_own, n_y)

    scores_t, _ = lax.optimization_barrier((scores_t, token_send))
    score_total = jnp.sum(scores_t, axis=0, keepdims=True)
    weights_t = ROUTE_SCALE * scores_t / score_total
    weight_of = jnp.sum(jnp.where(named, weights_t[:, None, :], 0.0), axis=0)
    weight_place = jnp.where(placed, weight_of[:, None, :], 0.0).reshape(slots, tok_count)
    row_weight = jnp.sum(weight_place, axis=1, keepdims=True)
    grad_rows = dot(place, out_grad)
    grad_send = (row_weight * grad_rows).astype(BF)
    grad_send, grad_rows = lax.optimization_barrier((grad_send, grad_rows.astype(BF)))
    grad_slab = exchange(grad_send)

    tok_part = permute_core(relative(token_slab, 1 - core, y, n_y), n_y)
    tok_own = relative(token_slab, core, y, n_y)
    near, got, _ = reduce_rows(dot, tok_own, tok_part, in_own, in_part, n_y)
    gate_up = add_all(near, got)
    gate, up = gate_up[:, :hidden_units], gate_up[:, hidden_units:]
    sig = jax.nn.sigmoid(gate)
    hidden = (gate * sig * up).astype(BF)
    factor = jnp.concatenate([up * sig * (1.0 + gate * (1.0 - sig)), gate * sig], axis=1)
    hidden, factor = lax.optimization_barrier((hidden, factor))
    hid_parts = [permute_y(hidden, -d, n_y) for d in range(1, n_y)]

    grad_slab, _ = lax.optimization_barrier((grad_slab, hidden))
    grad_part = permute_core(relative(grad_slab, 1 - core, y, n_y), n_y)
    grad_own = relative(grad_slab, core, y, n_y)
    near, got, sent = reduce_rows(dot_t, grad_own, grad_part, out_own, out_part, n_y)
    near, up_sum, dn_sum = lax.optimization_barrier((near, *got))
    gate_up_grad = gate_grad(near, up_sum, dn_sum, factor)

    hid_parts, _ = lax.optimization_barrier((hid_parts, sent))
    hid = jnp.concatenate([hidden] + hid_parts, axis=0)
    out_other = permute_core(absolute(dot(hid, out_part).astype(BF), y, n_y), n_y)
    out_mine = absolute(dot(hid, out_own).astype(BF), y, n_y)
    expert_out = both_halves(out_mine, out_other, core)
    out_back = exchange(expert_out)

    gug = gather_rows(gate_up_grad, n_y)
    grad_other = permute_core(absolute(dot_t(gug, in_part).astype(BF), y, n_y), n_y)
    grad_mine = absolute(dot_t(gug, in_own).astype(BF), y, n_y)
    choice_grad = both_halves(grad_mine, grad_other, core)
    grad_back = exchange(choice_grad)

    tok_part, tok_own, _ = lax.optimization_barrier((tok_part, tok_own, choice_grad))
    w_out_other = permute_core(gather_dot(hid, grad_part), n_y)
    w_out_grad = (gather_dot(hid, grad_own) + w_out_other).astype(BF)
    w_in_other = permute_core(gather_dot(tok_part, gug), n_y)
    w_in_grad = (gather_dot(tok_own, gug) + w_in_other).astype(BF)

    high = lax.reduce_precision(weight_place, 8, 7)
    low = (weight_place - high).astype(BF)
    high = high.astype(BF)
    layer_out = (gather_dot(high, out_back) + gather_dot(low, out_back)).astype(BF)
    slot_dot = jnp.sum(grad_rows.astype(F32) * out_back.astype(F32), axis=1)
    slot_dot = slot_dot.reshape(n_data, capacity)
    bit = 1
    while bit < 2 * n_y:
        slot_dot = slot_dot + permute_xor(slot_dot, bit, n_y)
        bit = 2 * bit
    dot_of = jnp.sum(jnp.where(placed, slot_dot[:, :, None], 0.0), axis=1)
    choice_dot = jnp.sum(jnp.where(named, dot_of[None, :, :], 0.0), axis=1)
    scores_grad = (
        ROUTE_SCALE * choice_dot - jnp.sum(choice_dot * weights_t, axis=0, keepdims=True)
    ) / score_total
    tokens_grad = gather_dot(place, grad_back).astype(BF)
    return layer_out, tokens_grad, scores_grad.T, w_in_grad[None], w_out_grad[None]


def solution(mesh):
    return jax.shard_map(
        body,
        mesh=mesh,
        in_specs=(
            P("dp", "expert"),
            P("dp", None),
            P("dp", None),
            P("dp", "expert", None),
            P("dp", None, "expert"),
            P("dp", "expert"),
        ),
        out_specs=(
            P("dp", "expert"),
            P("dp", "expert"),
            P("dp", None),
            P("dp", "expert", None),
            P("dp", None, "expert"),
        ),
        check_vma=False,
    )
```

```python
import jax
import jax.numpy as jnp
from jax import lax
from jax.experimental import pallas as pl
from jax.sharding import PartitionSpec as P


ROUTE_SCALE = 2.5
BF = jnp.bfloat16
F32 = jnp.float32


def permute_y(v, step, n_y):
    return lax.ppermute(
        v, "expert", [(2 * y + c, 2 * ((y + step) % n_y) + c) for y in range(n_y) for c in range(2)]
    )


def permute_core(v, n_y):
    return lax.ppermute(
        v, "expert", [(2 * y + c, 2 * y + 1 - c) for y in range(n_y) for c in range(2)]
    )


def dot(a, b):
    return jnp.dot(a, b, preferred_element_type=F32)


def dot_t(a, b):
    return jnp.einsum("rd,fd->rf", a, b, preferred_element_type=F32)


def gather_dot(a, b):
    return jnp.einsum("rd,rf->df", a, b, preferred_element_type=F32)


def permute_xor(v, bit, n_y):
    return lax.ppermute(v, "expert", [(e, e ^ bit) for e in range(2 * n_y)])


def reduce_rows(product, own, part, w_own, w_part, n_y):
    rows = own.shape[0] // n_y
    far = (product(own[rows:], w_own) + product(part[rows:], w_part)).astype(BF)
    got = [permute_y(far[(d - 1) * rows : d * rows], d, n_y) for d in range(1, n_y)]
    return product(own[:rows], w_own) + product(part[:rows], w_part), got


def reduce_rows_relayed(product, own, part, w_own, w_part, core, n_y):
    rows = own.shape[0] // n_y
    far = product(own[rows:], w_own) + product(part[rows:], w_part)
    b1, b2, b3 = far[:rows], far[rows : 2 * rows], far[2 * rows :]
    relay = permute_by_core(b2.astype(BF), n_y).astype(F32)
    up = (b1 + jnp.where(core == 0, relay, 0.0)).astype(BF)
    dn = (b3 + jnp.where(core == 0, 0.0, relay)).astype(BF)
    got = [permute_y(up, 1, n_y), permute_y(dn, -1, n_y)]
    return product(own[:rows], w_own) + product(part[:rows], w_part), got


def gate_grad_kernel(near, first, second, third, factor, out):
    width = near.shape[1]
    grad = near[...] + first[...].astype(F32) + second[...].astype(F32) + third[...].astype(F32)
    out[:, :width] = (grad * factor[:, :width]).astype(BF)
    out[:, width:] = (grad * factor[:, width:]).astype(BF)


def gate_grad(near, got, factor):
    rows, width = near.shape
    tile = rows // 2
    narrow = pl.BlockSpec((tile, width), lambda i: (i, 0))
    wide = pl.BlockSpec((tile, 2 * width), lambda i: (i, 0))
    return pl.pallas_call(
        gate_grad_kernel,
        grid=(2,),
        in_specs=[narrow, narrow, narrow, narrow, wide],
        out_specs=wide,
        out_shape=jax.ShapeDtypeStruct((rows, 2 * width), BF),
    )(near, *got, factor)


def permute_by_core(v, n_y):
    return lax.ppermute(
        v,
        "expert",
        [(2 * y + c, 2 * ((y + 1 - 2 * c) % n_y) + c) for y in range(n_y) for c in range(2)],
    )


def gather_rows(v, core, n_y):
    dn = permute_y(v, 1, n_y)
    up = permute_y(v, -1, n_y)
    far = permute_by_core(jnp.where(core == 0, dn, up), n_y)
    return jnp.concatenate([v, up, far, dn], axis=0)


def relative(slab, half, y, n_y):
    rows = slab.shape[0] // (2 * n_y)
    return jnp.concatenate(
        [
            lax.dynamic_slice_in_dim(slab, (half * n_y + (y + d) % n_y) * rows, rows, 0)
            for d in range(n_y)
        ],
        axis=0,
    )


def absolute(part, y, n_y):
    rows = part.shape[0] // n_y
    return jnp.concatenate(
        [lax.dynamic_slice_in_dim(part, ((yy - y) % n_y) * rows, rows, 0) for yy in range(n_y)],
        axis=0,
    )


def both_halves(own, other, core):
    flat = jnp.where(core == 0, jnp.stack([own, other]), jnp.stack([other, own]))
    return flat.reshape(2 * own.shape[0], own.shape[1])


def body(tokens, expert_ids, scores, weight_in, weight_out, out_grad):
    n_data = lax.axis_size("dp")
    n_y = lax.axis_size("expert") // 2
    here = lax.axis_index("expert")
    y, core = lax.div(here, 2), lax.rem(here, 2)
    tok_count, width = tokens.shape
    top_count = expert_ids.shape[1]
    hidden_units = weight_out.shape[1]
    capacity = min(tok_count, 5 * tok_count * top_count // (4 * n_data))
    slots = n_data * capacity

    ids_t = expert_ids.T
    scores_t = scores.T
    named = ids_t[:, None, :] == jnp.arange(n_data, dtype=jnp.int32)[None, :, None]
    hot = jnp.sum(named.astype(F32), axis=0)
    before = (
        jnp.arange(tok_count, dtype=jnp.int32)[:, None] < jnp.arange(tok_count, dtype=jnp.int32)[None, :]
    ).astype(BF)
    rank = dot(hot.astype(BF), before)
    position = jnp.where(hot > 0.0, rank, -1.0).astype(jnp.int32)
    placed = position[:, None, :] == jnp.arange(capacity, dtype=jnp.int32)[None, :, None]
    place = placed.astype(BF).reshape(slots, tok_count)

    token_send = dot(place, tokens).astype(BF)

    def exchange(v):
        v = v.reshape(n_data, capacity, width)
        return lax.all_to_all(v, "dp", split_axis=0, concat_axis=0, tiled=True).reshape(slots, width)

    in_own, out_own = weight_in[0], weight_out[0]
    token_slab = exchange(token_send)
    in_part = permute_core(in_own, n_y)
    out_part = permute_core(out_own, n_y)

    scores_t, _ = lax.optimization_barrier((scores_t, token_send))
    score_total = jnp.sum(scores_t, axis=0, keepdims=True)
    weights_t = ROUTE_SCALE * scores_t / score_total
    weight_of = jnp.sum(jnp.where(named, weights_t[:, None, :], 0.0), axis=0)
    weight_place = jnp.where(placed, weight_of[:, None, :], 0.0).reshape(slots, tok_count)
    row_weight = jnp.sum(weight_place, axis=1, keepdims=True)
    grad_rows = dot(place, out_grad)
    grad_send = (row_weight * grad_rows).astype(BF)
    grad_send, grad_rows = lax.optimization_barrier((grad_send, grad_rows.astype(BF)))
    grad_slab = exchange(grad_send)

    tok_part = permute_core(relative(token_slab, 1 - core, y, n_y), n_y)
    tok_own = relative(token_slab, core, y, n_y)
    near, got = reduce_rows_relayed(dot, tok_own, tok_part, in_own, in_part, core, n_y)
    gate_up = near
    for piece in got:
        gate_up = gate_up + piece.astype(F32)
    gate, up = gate_up[:, :hidden_units], gate_up[:, hidden_units:]
    hidden = (gate * jax.nn.sigmoid(gate) * up).astype(BF)
    hid_parts = [permute_y(hidden, -d, n_y) for d in range(1, n_y)]
    gate, up, _ = lax.optimization_barrier((gate, up, hidden))
    sig = jax.nn.sigmoid(gate)
    factor = jnp.concatenate([up * sig * (1.0 + gate * (1.0 - sig)), gate * sig], axis=1)

    grad_slab, _ = lax.optimization_barrier((grad_slab, hidden))
    grad_part = permute_core(relative(grad_slab, 1 - core, y, n_y), n_y)
    grad_own = relative(grad_slab, core, y, n_y)
    near, got = reduce_rows(dot_t, grad_own, grad_part, out_own, out_part, n_y)
    gate_up_grad = gate_grad(near, got, factor)

    hid = jnp.concatenate([hidden] + hid_parts, axis=0)
    out_other = permute_core(absolute(dot(hid, out_part).astype(BF), y, n_y), n_y)
    out_mine = absolute(dot(hid, out_own).astype(BF), y, n_y)
    expert_out = both_halves(out_mine, out_other, core)
    out_back = exchange(expert_out)

    gug = gather_rows(gate_up_grad, core, n_y)
    grad_other = permute_core(absolute(dot_t(gug, in_part).astype(BF), y, n_y), n_y)
    grad_mine = absolute(dot_t(gug, in_own).astype(BF), y, n_y)
    choice_grad = both_halves(grad_mine, grad_other, core)
    grad_back = exchange(choice_grad)

    tok_part, tok_own, _ = lax.optimization_barrier((tok_part, tok_own, choice_grad))
    w_out_other = permute_core(gather_dot(hid, grad_part), n_y)
    w_out_grad = (gather_dot(hid, grad_own) + w_out_other).astype(BF)
    w_in_other = permute_core(gather_dot(tok_part, gug), n_y)
    w_in_grad = (gather_dot(tok_own, gug) + w_in_other).astype(BF)

    high = lax.reduce_precision(weight_place, 8, 7)
    low = (weight_place - high).astype(BF)
    high = high.astype(BF)
    layer_out = (gather_dot(high, out_back) + gather_dot(low, out_back)).astype(BF)
    slot_dot = jnp.sum(grad_rows.astype(F32) * out_back.astype(F32), axis=1)
    slot_dot = slot_dot.reshape(n_data, capacity)
    bit = 1
    while bit < 2 * n_y:
        slot_dot = slot_dot + permute_xor(slot_dot, bit, n_y)
        bit = 2 * bit
    dot_of = jnp.sum(jnp.where(placed, slot_dot[:, :, None], 0.0), axis=1)
    choice_dot = jnp.sum(jnp.where(named, dot_of[None, :, :], 0.0), axis=1)
    scores_grad = (
        ROUTE_SCALE * choice_dot - jnp.sum(choice_dot * weights_t, axis=0, keepdims=True)
    ) / score_total
    tokens_grad = gather_dot(place, grad_back).astype(BF)
    return layer_out, tokens_grad, scores_grad.T, w_in_grad[None], w_out_grad[None]


def solution(mesh):
    return jax.shard_map(
        body,
        mesh=mesh,
        in_specs=(
            P("dp", "expert"),
            P("dp", None),
            P("dp", None),
            P("dp", "expert", None),
            P("dp", None, "expert"),
            P("dp", "expert"),
        ),
        out_specs=(
            P("dp", "expert"),
            P("dp", "expert"),
            P("dp", None),
            P("dp", "expert", None),
            P("dp", None, "expert"),
        ),
        check_vma=False,
    )
```

```python
import functools

import jax
import jax.numpy as jnp
from jax import lax
from jax.experimental import pallas as pl
from jax.experimental.pallas import tpu as pltpu
from jax.sharding import PartitionSpec as P


ROUTE_SCALE = 2.5
BF = jnp.bfloat16
F32 = jnp.float32


def permute_y(v, step, n_y):
    return lax.ppermute(
        v, "expert", [(2 * y + c, 2 * ((y + step) % n_y) + c) for y in range(n_y) for c in range(2)]
    )


def permute_core(v, n_y):
    return lax.ppermute(
        v, "expert", [(2 * y + c, 2 * y + 1 - c) for y in range(n_y) for c in range(2)]
    )


def dot(a, b):
    return jnp.dot(a, b, preferred_element_type=F32)


def dot_t(a, b):
    return jnp.einsum("rd,fd->rf", a, b, preferred_element_type=F32)


def gather_dot(a, b):
    return jnp.einsum("rd,rf->df", a, b, preferred_element_type=F32)


def permute_xor(v, bit, n_y):
    return lax.ppermute(v, "expert", [(e, e ^ bit) for e in range(2 * n_y)])


def partial_kernel(order, own, part, w_own, w_part, near, far1, far2, far3, *, dims, chunk):
    step = pl.program_id(0)
    width = near.shape[1]

    def columns(j, carry):
        cols = pl.ds(pl.multiple_of(j * chunk, chunk), chunk)
        if dims[1] == 0:
            a, b = w_own[:, cols], w_part[:, cols]
        else:
            a, b = w_own[cols, :], w_part[cols, :]
        contract = (((1,), (dims[1],)), ((), ()))
        total = lax.dot_general(own[...], a, contract, preferred_element_type=F32)
        total = total + lax.dot_general(part[...], b, contract, preferred_element_type=F32)
        for k, out in enumerate((far1, far2, far3)):

            @pl.when(step == k)
            def _(out=out):
                out[:, cols] = total.astype(BF)

        @pl.when(step == 3)
        def _():
            near[:, cols] = total

        return carry

    lax.fori_loop(0, width // chunk, columns, 0)


def partial_products(slab, part, w_own, w_part, order, turned):
    n_y = order.shape[0]
    rows = part.shape[0] // n_y
    k = slab.shape[1]
    width = w_own.shape[0] if turned else w_own.shape[1]
    whole = pl.BlockSpec(w_own.shape, lambda i, order: (0, 0))
    out = pl.BlockSpec((rows, width), lambda i, order: (0, 0))
    return pl.pallas_call(
        functools.partial(partial_kernel, dims=(1, 1 if turned else 0), chunk=512),
        grid_spec=pltpu.PrefetchScalarGridSpec(
            num_scalar_prefetch=1,
            grid=(n_y,),
            in_specs=[
                pl.BlockSpec((rows, k), lambda i, order: (order[i], 0)),
                pl.BlockSpec((rows, k), lambda i, order: ((i + 1) % 4, 0)),
                whole,
                whole,
            ],
            out_specs=[out, out, out, out],
        ),
        out_shape=[jax.ShapeDtypeStruct((rows, width), F32)]
        + [jax.ShapeDtypeStruct((rows, width), BF)] * 3,
    )(order, slab, part, w_own, w_part)


def send_far(far, n_y):
    return [permute_y(piece, d + 1, n_y) for d, piece in enumerate(far)]


def hidden_kernel(near, first, second, third, gate_up, hidden):
    width = hidden.shape[1]
    total = near[...] + first[...].astype(F32) + second[...].astype(F32) + third[...].astype(F32)
    gate_up[...] = total
    gate, up = total[:, :width], total[:, width:]
    hidden[...] = (gate * jax.nn.sigmoid(gate) * up).astype(BF)


def hidden_rows(near, got):
    rows, width = near.shape
    tile = rows // 2
    wide = pl.BlockSpec((tile, width), lambda i: (i, 0))
    return pl.pallas_call(
        hidden_kernel,
        grid=(2,),
        in_specs=[wide, wide, wide, wide],
        out_specs=[wide, pl.BlockSpec((tile, width // 2), lambda i: (i, 0))],
        out_shape=[
            jax.ShapeDtypeStruct((rows, width), F32),
            jax.ShapeDtypeStruct((rows, width // 2), BF),
        ],
    )(near, *got)


def gate_grad_kernel(near, first, second, third, gate_up, out):
    width = near.shape[1]
    grad = near[...] + first[...].astype(F32) + second[...].astype(F32) + third[...].astype(F32)
    gate, up = gate_up[:, :width], gate_up[:, width:]
    sig = jax.nn.sigmoid(gate)
    out[:, :width] = (grad * up * sig * (1.0 + gate * (1.0 - sig))).astype(BF)
    out[:, width:] = (grad * gate * sig).astype(BF)


def gate_grad(near, got, gate_up):
    rows, width = near.shape
    tile = rows // 2
    narrow = pl.BlockSpec((tile, width), lambda i: (i, 0))
    wide = pl.BlockSpec((tile, 2 * width), lambda i: (i, 0))
    return pl.pallas_call(
        gate_grad_kernel,
        grid=(2,),
        in_specs=[narrow, narrow, narrow, narrow, wide],
        out_specs=wide,
        out_shape=jax.ShapeDtypeStruct((rows, 2 * width), BF),
    )(near, *got, gate_up)


def permute_by_core(v, n_y):
    return lax.ppermute(
        v,
        "expert",
        [(2 * y + c, 2 * ((y + 1 - 2 * c) % n_y) + c) for y in range(n_y) for c in range(2)],
    )


def gather_rows(v, core, n_y):
    dn = permute_y(v, 1, n_y)
    up = permute_y(v, -1, n_y)
    far = permute_by_core(jnp.where(core == 0, dn, up), n_y)
    return jnp.concatenate([v, up, far, dn], axis=0)


def relative(slab, half, y, n_y):
    rows = slab.shape[0] // (2 * n_y)
    return jnp.concatenate(
        [
            lax.dynamic_slice_in_dim(slab, (half * n_y + (y + d) % n_y) * rows, rows, 0)
            for d in range(n_y)
        ],
        axis=0,
    )


def absolute(part, y, n_y):
    rows = part.shape[0] // n_y
    return jnp.concatenate(
        [lax.dynamic_slice_in_dim(part, ((yy - y) % n_y) * rows, rows, 0) for yy in range(n_y)],
        axis=0,
    )


def both_halves(own, other, core):
    flat = jnp.where(core == 0, jnp.stack([own, other]), jnp.stack([other, own]))
    return flat.reshape(2 * own.shape[0], own.shape[1])


def body(tokens, expert_ids, scores, weight_in, weight_out, out_grad):
    n_data = lax.axis_size("dp")
    n_y = lax.axis_size("expert") // 2
    here = lax.axis_index("expert")
    y, core = lax.div(here, 2), lax.rem(here, 2)
    tok_count, width = tokens.shape
    top_count = expert_ids.shape[1]
    capacity = min(tok_count, 5 * tok_count * top_count // (4 * n_data))
    slots = n_data * capacity

    ids_t = expert_ids.T
    scores_t = scores.T
    named = ids_t[:, None, :] == jnp.arange(n_data, dtype=jnp.int32)[None, :, None]
    hot = jnp.sum(named.astype(F32), axis=0)
    before = (
        jnp.arange(tok_count, dtype=jnp.int32)[:, None] < jnp.arange(tok_count, dtype=jnp.int32)[None, :]
    ).astype(BF)
    rank = dot(hot.astype(BF), before)
    position = jnp.where(hot > 0.0, rank, -1.0).astype(jnp.int32)
    placed = position[:, None, :] == jnp.arange(capacity, dtype=jnp.int32)[None, :, None]
    place = placed.astype(BF).reshape(slots, tok_count)

    token_send = dot(place, tokens).astype(BF)

    def exchange(v):
        v = v.reshape(n_data, capacity, width)
        return lax.all_to_all(v, "dp", split_axis=0, concat_axis=0, tiled=True).reshape(slots, width)

    in_own, out_own = weight_in[0], weight_out[0]
    token_slab = exchange(token_send)
    in_part = permute_core(in_own, n_y)
    out_part = permute_core(out_own, n_y)

    scores_t, _ = lax.optimization_barrier((scores_t, token_send))
    score_total = jnp.sum(scores_t, axis=0, keepdims=True)
    weights_t = ROUTE_SCALE * scores_t / score_total
    weight_of = jnp.sum(jnp.where(named, weights_t[:, None, :], 0.0), axis=0)
    weight_place = jnp.where(placed, weight_of[:, None, :], 0.0).reshape(slots, tok_count)
    row_weight = jnp.sum(weight_place, axis=1, keepdims=True)
    grad_rows = dot(place, out_grad)
    grad_send = (row_weight * grad_rows).astype(BF)
    grad_send, grad_rows = lax.optimization_barrier((grad_send, grad_rows.astype(BF)))
    grad_slab = exchange(grad_send)

    token_slab, _ = lax.optimization_barrier((token_slab, grad_send[:8]))
    order = core * n_y + lax.rem(y + jnp.array([1, 2, 3, 4], jnp.int32), n_y)
    tok_part = permute_core(relative(token_slab, 1 - core, y, n_y), n_y)
    near, *far = partial_products(token_slab, tok_part, in_own, in_part, order, False)
    got = send_far(far, n_y)
    gate_up, hidden = hidden_rows(near, got)
    hid_parts = [permute_y(hidden, -d, n_y) for d in range(1, n_y)]

    grad_slab, _ = lax.optimization_barrier((grad_slab, hidden))
    grad_part = permute_core(relative(grad_slab, 1 - core, y, n_y), n_y)
    near, *far = partial_products(grad_slab, grad_part, out_own, out_part, order, True)
    got = send_far(far, n_y)
    gate_up_grad = gate_grad(near, got, gate_up)
    grad_slab, _ = lax.optimization_barrier((grad_slab, gate_up_grad))
    grad_own = relative(grad_slab, core, y, n_y)
    token_slab, _ = lax.optimization_barrier((token_slab, gate_up_grad))
    tok_own = relative(token_slab, core, y, n_y)

    hid_parts, _ = lax.optimization_barrier((hid_parts, far[0]))
    hid = jnp.concatenate([hidden] + hid_parts, axis=0)
    out_other = permute_core(absolute(dot(hid, out_part).astype(BF), y, n_y), n_y)
    out_mine = absolute(dot(hid, out_own).astype(BF), y, n_y)
    expert_out = both_halves(out_mine, out_other, core)
    out_back = exchange(expert_out)

    gug = gather_rows(gate_up_grad, core, n_y)
    grad_other = permute_core(absolute(dot_t(gug, in_part).astype(BF), y, n_y), n_y)
    grad_mine = absolute(dot_t(gug, in_own).astype(BF), y, n_y)
    choice_grad = both_halves(grad_mine, grad_other, core)
    grad_back = exchange(choice_grad)

    tok_part, tok_own, _ = lax.optimization_barrier((tok_part, tok_own, choice_grad))
    w_out_other = permute_core(gather_dot(hid, grad_part), n_y)
    w_out_grad = (gather_dot(hid, grad_own) + w_out_other).astype(BF)
    w_in_other = permute_core(gather_dot(tok_part, gug), n_y)
    w_in_grad = (gather_dot(tok_own, gug) + w_in_other).astype(BF)

    high = lax.reduce_precision(weight_place, 8, 7)
    low = (weight_place - high).astype(BF)
    high = high.astype(BF)
    layer_out = (gather_dot(high, out_back) + gather_dot(low, out_back)).astype(BF)
    slot_dot = jnp.sum(grad_rows.astype(F32) * out_back.astype(F32), axis=1)
    slot_dot = slot_dot.reshape(n_data, capacity)
    bit = 1
    while bit < 2 * n_y:
        slot_dot = slot_dot + permute_xor(slot_dot, bit, n_y)
        bit = 2 * bit
    dot_of = jnp.sum(jnp.where(placed, slot_dot[:, :, None], 0.0), axis=1)
    choice_dot = jnp.sum(jnp.where(named, dot_of[None, :, :], 0.0), axis=1)
    scores_grad = (
        ROUTE_SCALE * choice_dot - jnp.sum(choice_dot * weights_t, axis=0, keepdims=True)
    ) / score_total
    tokens_grad = gather_dot(place, grad_back).astype(BF)
    return layer_out, tokens_grad, scores_grad.T, w_in_grad[None], w_out_grad[None]


def solution(mesh):
    return jax.shard_map(
        body,
        mesh=mesh,
        in_specs=(
            P("dp", "expert"),
            P("dp", None),
            P("dp", None),
            P("dp", "expert", None),
            P("dp", None, "expert"),
            P("dp", "expert"),
        ),
        out_specs=(
            P("dp", "expert"),
            P("dp", "expert"),
            P("dp", None),
            P("dp", "expert", None),
            P("dp", None, "expert"),
        ),
        check_vma=False,
    )
```

```python
import functools

import jax
import jax.numpy as jnp
from jax import lax
from jax.experimental import pallas as pl
from jax.experimental.pallas import tpu as pltpu
from jax.sharding import PartitionSpec as P


ROUTE_SCALE = 2.5
BF = jnp.bfloat16
F32 = jnp.float32


def permute_y(v, step, n_y):
    return lax.ppermute(
        v, "expert", [(2 * y + c, 2 * ((y + step) % n_y) + c) for y in range(n_y) for c in range(2)]
    )


def permute_core(v, n_y):
    return lax.ppermute(
        v, "expert", [(2 * y + c, 2 * y + 1 - c) for y in range(n_y) for c in range(2)]
    )


def dot(a, b):
    return jnp.dot(a, b, preferred_element_type=F32)


def gather_dot(a, b):
    return jnp.einsum("rd,rf->df", a, b, preferred_element_type=F32)


def permute_xor(v, bit, n_y):
    return lax.ppermute(v, "expert", [(e, e ^ bit) for e in range(2 * n_y)])


def partial_kernel(order, own0, own1, own2, own3, part, w_own, w_part, near, *far, turned):
    rows = near.shape[0]
    contract = (((1,), (1 if turned else 0,)), ((), ()))
    own = jnp.concatenate([own0[...], own1[...], own2[...], own3[...]], axis=0)
    total = lax.dot_general(own, w_own[...], contract, preferred_element_type=F32)
    total = total + lax.dot_general(part[...], w_part[...], contract, preferred_element_type=F32)
    near[...] = total[:rows]
    for k, out in enumerate(far):
        out[...] = total[(k + 1) * rows : (k + 2) * rows].astype(BF)


def partial_products(slab, part, w_own, w_part, order, turned):
    n_y = order.shape[0]
    rows = part.shape[0] // n_y
    k = slab.shape[1]
    width = w_own.shape[0] if turned else w_own.shape[1]
    chunk = width // 4

    def rows_of(d):
        return pl.BlockSpec((rows, k), lambda j, order: (order[d], 0))

    if turned:
        weight = pl.BlockSpec((chunk, k), lambda j, order: (j, 0))
    else:
        weight = pl.BlockSpec((k, chunk), lambda j, order: (0, j))
    out = pl.BlockSpec((rows, chunk), lambda j, order: (0, j))
    return pl.pallas_call(
        functools.partial(partial_kernel, turned=turned),
        grid_spec=pltpu.PrefetchScalarGridSpec(
            num_scalar_prefetch=1,
            grid=(width // chunk,),
            in_specs=[rows_of(d) for d in range(4)]
            + [pl.BlockSpec(part.shape, lambda j, order: (0, 0)), weight, weight],
            out_specs=[out, out, out, out],
        ),
        out_shape=[jax.ShapeDtypeStruct((rows, width), F32)]
        + [jax.ShapeDtypeStruct((rows, width), BF)] * 3,
    )(order, slab, slab, slab, slab, part, w_own, w_part)


def spread_kernel(places, p0, p1, p2, p3, weight, out, held, *, turned):
    rows = p0.shape[0]

    @pl.when(pl.program_id(0) == 0)
    def _():
        for d, piece in enumerate((p0, p1, p2, p3)):
            held[d * rows : (d + 1) * rows, :] = piece[...]

    contract = (((1,), (1 if turned else 0,)), ((), ()))
    total = lax.dot_general(held[...], weight[...], contract, preferred_element_type=F32).astype(BF)
    for d in range(4):
        start = pl.multiple_of(places[d] * rows, rows)
        out[pl.ds(start, rows), :] = total[d * rows : (d + 1) * rows]


def spread_product(pieces, weight, places, turned):
    rows, k = pieces[0].shape
    width = weight.shape[0] if turned else weight.shape[1]
    chunk = width // 2
    piece = pl.BlockSpec((rows, k), lambda j, places: (0, 0))
    if turned:
        w_spec = pl.BlockSpec((chunk, k), lambda j, places: (j, 0))
    else:
        w_spec = pl.BlockSpec((k, chunk), lambda j, places: (0, j))
    return pl.pallas_call(
        functools.partial(spread_kernel, turned=turned),
        grid_spec=pltpu.PrefetchScalarGridSpec(
            num_scalar_prefetch=1,
            grid=(2,),
            in_specs=[piece, piece, piece, piece, w_spec],
            out_specs=pl.BlockSpec((4 * rows, chunk), lambda j, places: (0, j)),
            scratch_shapes=[pltpu.VMEM((4 * rows, k), BF)],
        ),
        out_shape=jax.ShapeDtypeStruct((4 * rows, width), BF),
    )(places, *pieces, weight)


def send_far(far, n_y):
    return [permute_y(piece, d + 1, n_y) for d, piece in enumerate(far)]


def hidden_kernel(near, first, second, third, gate_up, hidden):
    width = hidden.shape[1]
    total = near[...] + first[...].astype(F32) + second[...].astype(F32) + third[...].astype(F32)
    gate_up[...] = total
    gate, up = total[:, :width], total[:, width:]
    hidden[...] = (gate * jax.nn.sigmoid(gate) * up).astype(BF)


def hidden_rows(near, got):
    rows, width = near.shape
    tile = rows // 2
    wide = pl.BlockSpec((tile, width), lambda i: (i, 0))
    return pl.pallas_call(
        hidden_kernel,
        grid=(2,),
        in_specs=[wide, wide, wide, wide],
        out_specs=[wide, pl.BlockSpec((tile, width // 2), lambda i: (i, 0))],
        out_shape=[
            jax.ShapeDtypeStruct((rows, width), F32),
            jax.ShapeDtypeStruct((rows, width // 2), BF),
        ],
    )(near, *got)


def gate_grad_kernel(near, first, second, third, gate_up, out):
    width = near.shape[1]
    grad = near[...] + first[...].astype(F32) + second[...].astype(F32) + third[...].astype(F32)
    gate, up = gate_up[:, :width], gate_up[:, width:]
    sig = jax.nn.sigmoid(gate)
    out[:, :width] = (grad * up * sig * (1.0 + gate * (1.0 - sig))).astype(BF)
    out[:, width:] = (grad * gate * sig).astype(BF)


def gate_grad(near, got, gate_up):
    rows, width = near.shape
    tile = rows // 2
    narrow = pl.BlockSpec((tile, width), lambda i: (i, 0))
    wide = pl.BlockSpec((tile, 2 * width), lambda i: (i, 0))
    return pl.pallas_call(
        gate_grad_kernel,
        grid=(2,),
        in_specs=[narrow, narrow, narrow, narrow, wide],
        out_specs=wide,
        out_shape=jax.ShapeDtypeStruct((rows, 2 * width), BF),
    )(near, *got, gate_up)


def permute_by_core(v, n_y):
    return lax.ppermute(
        v,
        "expert",
        [(2 * y + c, 2 * ((y + 1 - 2 * c) % n_y) + c) for y in range(n_y) for c in range(2)],
    )


def gather_rows(v, core, n_y):
    dn = permute_y(v, 1, n_y)
    up = permute_y(v, -1, n_y)
    far = permute_by_core(jnp.where(core == 0, dn, up), n_y)
    return [v, up, far, dn]


def relative(slab, half, y, n_y):
    rows = slab.shape[0] // (2 * n_y)
    return jnp.concatenate(
        [
            lax.dynamic_slice_in_dim(slab, (half * n_y + (y + d) % n_y) * rows, rows, 0)
            for d in range(n_y)
        ],
        axis=0,
    )


def both_halves(own, other, core):
    flat = jnp.where(core == 0, jnp.stack([own, other]), jnp.stack([other, own]))
    return flat.reshape(2 * own.shape[0], own.shape[1])


def body(tokens, expert_ids, scores, weight_in, weight_out, out_grad):
    n_data = lax.axis_size("dp")
    n_y = lax.axis_size("expert") // 2
    here = lax.axis_index("expert")
    y, core = lax.div(here, 2), lax.rem(here, 2)
    tok_count, width = tokens.shape
    top_count = expert_ids.shape[1]
    capacity = min(tok_count, 5 * tok_count * top_count // (4 * n_data))
    slots = n_data * capacity

    ids_t = expert_ids.T
    scores_t = scores.T
    named = ids_t[:, None, :] == jnp.arange(n_data, dtype=jnp.int32)[None, :, None]
    hot = jnp.sum(named.astype(F32), axis=0)
    before = (
        jnp.arange(tok_count, dtype=jnp.int32)[:, None] < jnp.arange(tok_count, dtype=jnp.int32)[None, :]
    ).astype(BF)
    rank = dot(hot.astype(BF), before)
    position = jnp.where(hot > 0.0, rank, -1.0).astype(jnp.int32)
    placed = position[:, None, :] == jnp.arange(capacity, dtype=jnp.int32)[None, :, None]
    place = placed.astype(BF).reshape(slots, tok_count)

    token_send = dot(place, tokens).astype(BF)

    def exchange(v):
        v = v.reshape(n_data, capacity, width)
        return lax.all_to_all(v, "dp", split_axis=0, concat_axis=0, tiled=True).reshape(slots, width)

    in_own, out_own = weight_in[0], weight_out[0]
    token_slab = exchange(token_send)
    in_part = permute_core(in_own, n_y)
    out_part = permute_core(out_own, n_y)

    places = lax.rem(y + jnp.arange(n_y, dtype=jnp.int32), n_y)
    order = core * n_y + places
    scores_t, places, order, _ = lax.optimization_barrier((scores_t, places, order, token_send))
    score_total = jnp.sum(scores_t, axis=0, keepdims=True)
    weights_t = ROUTE_SCALE * scores_t / score_total
    weight_of = jnp.sum(jnp.where(named, weights_t[:, None, :], 0.0), axis=0)
    weight_place = jnp.where(placed, weight_of[:, None, :], 0.0).reshape(slots, tok_count)
    row_weight = jnp.sum(weight_place, axis=1, keepdims=True)
    grad_rows = dot(place, out_grad)
    grad_send = (row_weight * grad_rows).astype(BF)
    grad_send, grad_rows = lax.optimization_barrier((grad_send, grad_rows.astype(BF)))
    grad_slab = exchange(grad_send)

    token_slab, _ = lax.optimization_barrier((token_slab, grad_send[:8]))
    tok_part = permute_core(relative(token_slab, 1 - core, y, n_y), n_y)
    near, *far = partial_products(token_slab, tok_part, in_own, in_part, order, False)
    got = send_far(far, n_y)
    gate_up, hidden = hidden_rows(near, got)
    hid_parts = [permute_y(hidden, -d, n_y) for d in range(1, n_y)]

    grad_slab, _ = lax.optimization_barrier((grad_slab, hidden))
    grad_part = permute_core(relative(grad_slab, 1 - core, y, n_y), n_y)
    near, *far = partial_products(grad_slab, grad_part, out_own, out_part, order, True)
    got = send_far(far, n_y)
    gate_up_grad = gate_grad(near, got, gate_up)
    grad_slab, _ = lax.optimization_barrier((grad_slab, gate_up_grad))
    grad_own = relative(grad_slab, core, y, n_y)
    token_slab, _ = lax.optimization_barrier((token_slab, gate_up_grad))
    tok_own = relative(token_slab, core, y, n_y)

    out_other = permute_core(spread_product([hidden] + hid_parts, out_part, places, False), n_y)
    out_mine = spread_product([hidden] + hid_parts, out_own, places, False)
    expert_out = both_halves(out_mine, out_other, core)
    out_back = exchange(expert_out)

    gug_parts = gather_rows(gate_up_grad, core, n_y)
    grad_other = permute_core(spread_product(gug_parts, in_part, places, True), n_y)
    grad_mine = spread_product(gug_parts, in_own, places, True)
    hidden, hid_parts, _ = lax.optimization_barrier((hidden, hid_parts, gate_up_grad))
    hid = jnp.concatenate([hidden] + hid_parts, axis=0)
    choice_grad = both_halves(grad_mine, grad_other, core)
    gug_parts, _ = lax.optimization_barrier((gug_parts, choice_grad))
    gug = jnp.concatenate(gug_parts, axis=0)
    grad_back = exchange(choice_grad)

    tok_part, tok_own, _ = lax.optimization_barrier((tok_part, tok_own, choice_grad))
    w_out_other = permute_core(gather_dot(hid, grad_part), n_y)
    w_out_grad = (gather_dot(hid, grad_own) + w_out_other).astype(BF)
    w_in_other = permute_core(gather_dot(tok_part, gug), n_y)
    w_in_grad = (gather_dot(tok_own, gug) + w_in_other).astype(BF)

    high = lax.reduce_precision(weight_place, 8, 7)
    low = (weight_place - high).astype(BF)
    high = high.astype(BF)
    layer_out = (gather_dot(high, out_back) + gather_dot(low, out_back)).astype(BF)
    slot_dot = jnp.sum(grad_rows.astype(F32) * out_back.astype(F32), axis=1)
    slot_dot = slot_dot.reshape(n_data, capacity)
    bit = 1
    while bit < 2 * n_y:
        slot_dot = slot_dot + permute_xor(slot_dot, bit, n_y)
        bit = 2 * bit
    dot_of = jnp.sum(jnp.where(placed, slot_dot[:, :, None], 0.0), axis=1)
    choice_dot = jnp.sum(jnp.where(named, dot_of[None, :, :], 0.0), axis=1)
    scores_grad = (
        ROUTE_SCALE * choice_dot - jnp.sum(choice_dot * weights_t, axis=0, keepdims=True)
    ) / score_total
    tokens_grad = gather_dot(place, grad_back).astype(BF)
    return layer_out, tokens_grad, scores_grad.T, w_in_grad[None], w_out_grad[None]


def solution(mesh):
    return jax.shard_map(
        body,
        mesh=mesh,
        in_specs=(
            P("dp", "expert"),
            P("dp", None),
            P("dp", None),
            P("dp", "expert", None),
            P("dp", None, "expert"),
            P("dp", "expert"),
        ),
        out_specs=(
            P("dp", "expert"),
            P("dp", "expert"),
            P("dp", None),
            P("dp", "expert", None),
            P("dp", None, "expert"),
        ),
        check_vma=False,
    )
```

```python
import functools

import jax
import jax.numpy as jnp
from jax import lax
from jax.experimental import pallas as pl
from jax.experimental.pallas import tpu as pltpu
from jax.sharding import PartitionSpec as P


ROUTE_SCALE = 2.5
BF = jnp.bfloat16
F32 = jnp.float32


def permute_y(v, step, n_y):
    return lax.ppermute(
        v, "expert", [(2 * y + c, 2 * ((y + step) % n_y) + c) for y in range(n_y) for c in range(2)]
    )


def permute_core(v, n_y):
    return lax.ppermute(
        v, "expert", [(2 * y + c, 2 * y + 1 - c) for y in range(n_y) for c in range(2)]
    )


def dot(a, b):
    return jnp.dot(a, b, preferred_element_type=F32)


def dot_t(a, b):
    return jnp.einsum("rd,fd->rf", a, b, preferred_element_type=F32)


def gather_dot(a, b):
    return jnp.einsum("rd,rf->df", a, b, preferred_element_type=F32)


def permute_xor(v, bit, n_y):
    return lax.ppermute(v, "expert", [(e, e ^ bit) for e in range(2 * n_y)])


def partial_kernel(order, own0, own1, own2, own3, part, w_own, w_part, near, *far, turned):
    rows = near.shape[0]
    contract = (((1,), (1 if turned else 0,)), ((), ()))
    own = jnp.concatenate([own0[...], own1[...], own2[...], own3[...]], axis=0)
    total = lax.dot_general(own, w_own[...], contract, preferred_element_type=F32)
    total = total + lax.dot_general(part[...], w_part[...], contract, preferred_element_type=F32)
    near[...] = total[:rows]
    for k, out in enumerate(far):
        out[...] = total[(k + 1) * rows : (k + 2) * rows].astype(BF)


def partial_products(slab, part, w_own, w_part, order, turned):
    n_y = order.shape[0]
    rows = part.shape[0] // n_y
    k = slab.shape[1]
    width = w_own.shape[0] if turned else w_own.shape[1]
    chunk = width // 4

    def rows_of(d):
        return pl.BlockSpec((rows, k), lambda j, order: (order[d], 0))

    if turned:
        weight = pl.BlockSpec((chunk, k), lambda j, order: (j, 0))
    else:
        weight = pl.BlockSpec((k, chunk), lambda j, order: (0, j))
    out = pl.BlockSpec((rows, chunk), lambda j, order: (0, j))
    return pl.pallas_call(
        functools.partial(partial_kernel, turned=turned),
        grid_spec=pltpu.PrefetchScalarGridSpec(
            num_scalar_prefetch=1,
            grid=(width // chunk,),
            in_specs=[rows_of(d) for d in range(4)]
            + [pl.BlockSpec(part.shape, lambda j, order: (0, 0)), weight, weight],
            out_specs=[out, out, out, out],
        ),
        out_shape=[jax.ShapeDtypeStruct((rows, width), F32)]
        + [jax.ShapeDtypeStruct((rows, width), BF)] * 3,
    )(order, slab, slab, slab, slab, part, w_own, w_part)


def spread_kernel(places, p0, p1, p2, p3, weight, out, held, *, turned):
    rows = p0.shape[0]

    @pl.when(pl.program_id(0) == 0)
    def _():
        for d, piece in enumerate((p0, p1, p2, p3)):
            held[d * rows : (d + 1) * rows, :] = piece[...]

    contract = (((1,), (1 if turned else 0,)), ((), ()))
    total = lax.dot_general(held[...], weight[...], contract, preferred_element_type=F32).astype(BF)
    for d in range(4):
        start = pl.multiple_of(places[d] * rows, rows)
        out[pl.ds(start, rows), :] = total[d * rows : (d + 1) * rows]


def spread_product(pieces, weight, places, turned):
    rows, k = pieces[0].shape
    width = weight.shape[0] if turned else weight.shape[1]
    chunk = width // 2
    piece = pl.BlockSpec((rows, k), lambda j, places: (0, 0))
    if turned:
        w_spec = pl.BlockSpec((chunk, k), lambda j, places: (j, 0))
    else:
        w_spec = pl.BlockSpec((k, chunk), lambda j, places: (0, j))
    return pl.pallas_call(
        functools.partial(spread_kernel, turned=turned),
        grid_spec=pltpu.PrefetchScalarGridSpec(
            num_scalar_prefetch=1,
            grid=(2,),
            in_specs=[piece, piece, piece, piece, w_spec],
            out_specs=pl.BlockSpec((4 * rows, chunk), lambda j, places: (0, j)),
            scratch_shapes=[pltpu.VMEM((4 * rows, k), BF)],
        ),
        out_shape=jax.ShapeDtypeStruct((4 * rows, width), BF),
    )(places, *pieces, weight)


def send_far(far, n_y):
    return [permute_y(piece, d + 1, n_y) for d, piece in enumerate(far)]


def hidden_kernel(near, first, second, third, gate_up, hidden):
    width = hidden.shape[1]
    total = near[...] + first[...].astype(F32) + second[...].astype(F32) + third[...].astype(F32)
    gate_up[...] = total
    gate, up = total[:, :width], total[:, width:]
    hidden[...] = (gate * jax.nn.sigmoid(gate) * up).astype(BF)


def hidden_rows(near, got):
    rows, width = near.shape
    tile = rows // 2
    wide = pl.BlockSpec((tile, width), lambda i: (i, 0))
    return pl.pallas_call(
        hidden_kernel,
        grid=(2,),
        in_specs=[wide, wide, wide, wide],
        out_specs=[wide, pl.BlockSpec((tile, width // 2), lambda i: (i, 0))],
        out_shape=[
            jax.ShapeDtypeStruct((rows, width), F32),
            jax.ShapeDtypeStruct((rows, width // 2), BF),
        ],
    )(near, *got)


def gate_grad_kernel(near, first, second, third, gate_up, out):
    width = near.shape[1]
    grad = near[...] + first[...].astype(F32) + second[...].astype(F32) + third[...].astype(F32)
    gate, up = gate_up[:, :width], gate_up[:, width:]
    sig = jax.nn.sigmoid(gate)
    out[:, :width] = (grad * up * sig * (1.0 + gate * (1.0 - sig))).astype(BF)
    out[:, width:] = (grad * gate * sig).astype(BF)


def gate_grad(near, got, gate_up):
    rows, width = near.shape
    tile = rows // 2
    narrow = pl.BlockSpec((tile, width), lambda i: (i, 0))
    wide = pl.BlockSpec((tile, 2 * width), lambda i: (i, 0))
    return pl.pallas_call(
        gate_grad_kernel,
        grid=(2,),
        in_specs=[narrow, narrow, narrow, narrow, wide],
        out_specs=wide,
        out_shape=jax.ShapeDtypeStruct((rows, 2 * width), BF),
    )(near, *got, gate_up)


def permute_by_core(v, n_y):
    return lax.ppermute(
        v,
        "expert",
        [(2 * y + c, 2 * ((y + 1 - 2 * c) % n_y) + c) for y in range(n_y) for c in range(2)],
    )


def gather_rows(v, core, n_y):
    dn = permute_y(v, 1, n_y)
    up = permute_y(v, -1, n_y)
    far = permute_by_core(jnp.where(core == 0, dn, up), n_y)
    return [v, up, far, dn]


def relative(slab, half, y, n_y):
    rows = slab.shape[0] // (2 * n_y)
    return jnp.concatenate(
        [
            lax.dynamic_slice_in_dim(slab, (half * n_y + (y + d) % n_y) * rows, rows, 0)
            for d in range(n_y)
        ],
        axis=0,
    )


def absolute(part, y, n_y):
    rows = part.shape[0] // n_y
    return jnp.concatenate(
        [lax.dynamic_slice_in_dim(part, ((yy - y) % n_y) * rows, rows, 0) for yy in range(n_y)],
        axis=0,
    )


def both_halves(own, other, core):
    flat = jnp.where(core == 0, jnp.stack([own, other]), jnp.stack([other, own]))
    return flat.reshape(2 * own.shape[0], own.shape[1])


def body(tokens, expert_ids, scores, weight_in, weight_out, out_grad):
    n_data = lax.axis_size("dp")
    n_y = lax.axis_size("expert") // 2
    here = lax.axis_index("expert")
    y, core = lax.div(here, 2), lax.rem(here, 2)
    tok_count, width = tokens.shape
    top_count = expert_ids.shape[1]
    capacity = min(tok_count, 5 * tok_count * top_count // (4 * n_data))
    slots = n_data * capacity

    ids_t = expert_ids.T
    scores_t = scores.T
    named = ids_t[:, None, :] == jnp.arange(n_data, dtype=jnp.int32)[None, :, None]
    hot = jnp.sum(named.astype(F32), axis=0)
    before = (
        jnp.arange(tok_count, dtype=jnp.int32)[:, None] < jnp.arange(tok_count, dtype=jnp.int32)[None, :]
    ).astype(BF)
    rank = dot(hot.astype(BF), before)
    position = jnp.where(hot > 0.0, rank, -1.0).astype(jnp.int32)
    placed = position[:, None, :] == jnp.arange(capacity, dtype=jnp.int32)[None, :, None]
    place = placed.astype(BF).reshape(slots, tok_count)

    token_send = dot(place, tokens).astype(BF)

    def exchange(v):
        v = v.reshape(n_data, capacity, width)
        return lax.all_to_all(v, "dp", split_axis=0, concat_axis=0, tiled=True).reshape(slots, width)

    in_own, out_own = weight_in[0], weight_out[0]
    token_slab = exchange(token_send)
    in_part = permute_core(in_own, n_y)
    out_part = permute_core(out_own, n_y)

    places = lax.rem(y + jnp.arange(n_y, dtype=jnp.int32), n_y)
    order = core * n_y + places
    scores_t, places, order, _ = lax.optimization_barrier((scores_t, places, order, token_send))
    score_total = jnp.sum(scores_t, axis=0, keepdims=True)
    weights_t = ROUTE_SCALE * scores_t / score_total
    weight_of = jnp.sum(jnp.where(named, weights_t[:, None, :], 0.0), axis=0)
    weight_place = jnp.where(placed, weight_of[:, None, :], 0.0).reshape(slots, tok_count)
    row_weight = jnp.sum(weight_place, axis=1, keepdims=True)
    grad_rows = dot(place, out_grad)
    grad_send = (row_weight * grad_rows).astype(BF)
    grad_send, grad_rows = lax.optimization_barrier((grad_send, grad_rows.astype(BF)))
    grad_slab = exchange(grad_send)

    token_slab, _ = lax.optimization_barrier((token_slab, grad_send[:8]))
    tok_part = permute_core(relative(token_slab, 1 - core, y, n_y), n_y)
    near, *far = partial_products(token_slab, tok_part, in_own, in_part, order, False)
    got = send_far(far, n_y)
    gate_up, hidden = hidden_rows(near, got)
    hid_parts = [permute_y(hidden, -d, n_y) for d in range(1, n_y)]

    grad_part = permute_core(relative(grad_slab, 1 - core, y, n_y), n_y)
    near, *far = partial_products(grad_slab, grad_part, out_own, out_part, order, True)
    got = send_far(far, n_y)
    gate_up_grad = gate_grad(near, got, gate_up)
    grad_slab, _ = lax.optimization_barrier((grad_slab, gate_up_grad))
    grad_own = relative(grad_slab, core, y, n_y)
    token_slab, _ = lax.optimization_barrier((token_slab, gate_up_grad))
    tok_own = relative(token_slab, core, y, n_y)

    out_other = permute_core(spread_product([hidden] + hid_parts, out_part, places, False), n_y)
    out_mine = spread_product([hidden] + hid_parts, out_own, places, False)
    expert_out = both_halves(out_mine, out_other, core)
    out_back = exchange(expert_out)

    gug = jnp.concatenate(gather_rows(gate_up_grad, core, n_y), axis=0)
    grad_other = permute_core(absolute(dot_t(gug, in_part).astype(BF), y, n_y), n_y)
    grad_mine = absolute(dot_t(gug, in_own).astype(BF), y, n_y)
    hidden, hid_parts, _ = lax.optimization_barrier((hidden, hid_parts, gate_up_grad))
    hid = jnp.concatenate([hidden] + hid_parts, axis=0)
    choice_grad = both_halves(grad_mine, grad_other, core)
    grad_back = exchange(choice_grad)

    tok_part, tok_own, _ = lax.optimization_barrier((tok_part, tok_own, choice_grad))
    w_out_other = permute_core(gather_dot(hid, grad_part), n_y)
    w_out_grad = (gather_dot(hid, grad_own) + w_out_other).astype(BF)
    w_in_other = permute_core(gather_dot(tok_part, gug), n_y)
    w_in_grad = (gather_dot(tok_own, gug) + w_in_other).astype(BF)

    high = lax.reduce_precision(weight_place, 8, 7)
    low = (weight_place - high).astype(BF)
    high = high.astype(BF)
    layer_out = (gather_dot(high, out_back) + gather_dot(low, out_back)).astype(BF)
    slot_dot = jnp.sum(grad_rows.astype(F32) * out_back.astype(F32), axis=1)
    slot_dot = slot_dot.reshape(n_data, capacity)
    bit = 1
    while bit < 2 * n_y:
        slot_dot = slot_dot + permute_xor(slot_dot, bit, n_y)
        bit = 2 * bit
    dot_of = jnp.sum(jnp.where(placed, slot_dot[:, :, None], 0.0), axis=1)
    choice_dot = jnp.sum(jnp.where(named, dot_of[None, :, :], 0.0), axis=1)
    scores_grad = (
        ROUTE_SCALE * choice_dot - jnp.sum(choice_dot * weights_t, axis=0, keepdims=True)
    ) / score_total
    tokens_grad = gather_dot(place, grad_back).astype(BF)
    return layer_out, tokens_grad, scores_grad.T, w_in_grad[None], w_out_grad[None]


def solution(mesh):
    return jax.shard_map(
        body,
        mesh=mesh,
        in_specs=(
            P("dp", "expert"),
            P("dp", None),
            P("dp", None),
            P("dp", "expert", None),
            P("dp", None, "expert"),
            P("dp", "expert"),
        ),
        out_specs=(
            P("dp", "expert"),
            P("dp", "expert"),
            P("dp", None),
            P("dp", "expert", None),
            P("dp", None, "expert"),
        ),
        check_vma=False,
    )
```

```python
import functools

import jax
import jax.numpy as jnp
from jax import lax
from jax.experimental import pallas as pl
from jax.experimental.pallas import tpu as pltpu
from jax.sharding import PartitionSpec as P


ROUTE_SCALE = 2.5
BF = jnp.bfloat16
F32 = jnp.float32


def permute_y(v, step, n_y):
    return lax.ppermute(
        v,
        "expert",
        [(2 * y + c, 2 * ((y + (2 * c - 1) * step) % n_y) + c) for y in range(n_y) for c in range(2)],
    )


def permute_core(v, n_y):
    return lax.ppermute(
        v, "expert", [(2 * y + c, 2 * y + 1 - c) for y in range(n_y) for c in range(2)]
    )


def dot(a, b):
    return jnp.dot(a, b, preferred_element_type=F32)


def dot_t(a, b):
    return jnp.einsum("rd,fd->rf", a, b, preferred_element_type=F32)


def gather_dot(a, b):
    return jnp.einsum("rd,rf->df", a, b, preferred_element_type=F32)


def permute_xor(v, bit, n_y):
    return lax.ppermute(v, "expert", [(e, e ^ bit) for e in range(2 * n_y)])


def partial_kernel(order, own0, own1, own2, own3, part, w_own, w_part, near, *far, turned):
    rows = near.shape[0]
    contract = (((1,), (1 if turned else 0,)), ((), ()))
    own = jnp.concatenate([own0[...], own1[...], own2[...], own3[...]], axis=0)
    total = lax.dot_general(own, w_own[...], contract, preferred_element_type=F32)
    total = total + lax.dot_general(part[...], w_part[...], contract, preferred_element_type=F32)
    near[...] = total[:rows]
    for k, out in enumerate(far):
        out[...] = total[(k + 1) * rows : (k + 2) * rows].astype(BF)


def partial_products(slab, part, w_own, w_part, order, turned):
    n_y = order.shape[0]
    rows = part.shape[0] // n_y
    k = slab.shape[1]
    width = w_own.shape[0] if turned else w_own.shape[1]
    chunk = width // 4

    def rows_of(d):
        return pl.BlockSpec((rows, k), lambda j, order: (order[d], 0))

    if turned:
        weight = pl.BlockSpec((chunk, k), lambda j, order: (j, 0))
    else:
        weight = pl.BlockSpec((k, chunk), lambda j, order: (0, j))
    out = pl.BlockSpec((rows, chunk), lambda j, order: (0, j))
    return pl.pallas_call(
        functools.partial(partial_kernel, turned=turned),
        grid_spec=pltpu.PrefetchScalarGridSpec(
            num_scalar_prefetch=1,
            grid=(width // chunk,),
            in_specs=[rows_of(d) for d in range(4)]
            + [pl.BlockSpec(part.shape, lambda j, order: (0, 0)), weight, weight],
            out_specs=[out, out, out, out],
        ),
        out_shape=[jax.ShapeDtypeStruct((rows, width), F32)]
        + [jax.ShapeDtypeStruct((rows, width), BF)] * 3,
    )(order, slab, slab, slab, slab, part, w_own, w_part)


def halves_kernel(order, own0, own1, own2, own3, part, w_own, w_part, near, *far):
    rows = near.shape[0]
    half = rows // 2
    own = jnp.concatenate([own0[...], own1[...], own2[...], own3[...]], axis=0)
    total = jnp.dot(own, w_own[...], preferred_element_type=F32)
    total = total + jnp.dot(part[...], w_part[...], preferred_element_type=F32)
    near[...] = total[:rows]
    for k, out in enumerate(far):
        out[...] = total[rows + k * half : rows + (k + 1) * half].astype(out.dtype)


def partial_halves(slab, part, w_own, w_part, order):
    n_y = order.shape[0]
    rows = part.shape[0] // n_y
    k = slab.shape[1]
    width = w_own.shape[1]
    chunk = width // 4

    def rows_of(d):
        return pl.BlockSpec((rows, k), lambda j, order: (order[d], 0))

    weight = pl.BlockSpec((k, chunk), lambda j, order: (0, j))
    half = pl.BlockSpec((rows // 2, chunk), lambda j, order: (0, j))
    kinds = [F32, BF, BF, BF, BF, F32]
    return pl.pallas_call(
        halves_kernel,
        grid_spec=pltpu.PrefetchScalarGridSpec(
            num_scalar_prefetch=1,
            grid=(width // chunk,),
            in_specs=[rows_of(d) for d in range(4)]
            + [pl.BlockSpec(part.shape, lambda j, order: (0, 0)), weight, weight],
            out_specs=[pl.BlockSpec((rows, chunk), lambda j, order: (0, j))] + [half] * 6,
        ),
        out_shape=[jax.ShapeDtypeStruct((rows, width), F32)]
        + [jax.ShapeDtypeStruct((rows // 2, width), kind) for kind in kinds],
    )(order, slab, slab, slab, slab, part, w_own, w_part)


def send_far(far, n_y):
    return [permute_y(piece, d + 1, n_y) for d, piece in enumerate(far)]


def hidden_kernel(near, up_a, dn_a, up_b, dn_b, gate_up, hidden):
    half, width = up_a.shape
    for k, (up, dn) in enumerate(((up_a, dn_a), (up_b, dn_b))):
        rows = pl.ds(k * half, half)
        total = near[rows, :] + up[...].astype(F32) + dn[...].astype(F32)
        gate_up[rows, :] = total
        gate, upward = total[:, : width // 2], total[:, width // 2 :]
        hidden[rows, :] = gate * jax.nn.sigmoid(gate) * upward


def hidden_rows(near, got):
    rows, width = near.shape
    return pl.pallas_call(
        hidden_kernel,
        out_shape=[
            jax.ShapeDtypeStruct((rows, width), F32),
            jax.ShapeDtypeStruct((rows, width // 2), F32),
        ],
    )(near, *got)


def gate_grad_kernel(near, first, second, third, gate_up, out):
    width = near.shape[1]
    grad = near[...] + first[...].astype(F32) + second[...].astype(F32) + third[...].astype(F32)
    gate, up = gate_up[:, :width], gate_up[:, width:]
    sig = jax.nn.sigmoid(gate)
    out[:, :width] = (grad * up * sig * (1.0 + gate * (1.0 - sig))).astype(BF)
    out[:, width:] = (grad * gate * sig).astype(BF)


def gate_grad(near, got, gate_up):
    rows, width = near.shape
    tile = rows // 2
    narrow = pl.BlockSpec((tile, width), lambda i: (i, 0))
    wide = pl.BlockSpec((tile, 2 * width), lambda i: (i, 0))
    return pl.pallas_call(
        gate_grad_kernel,
        grid=(2,),
        in_specs=[narrow, narrow, narrow, narrow, wide],
        out_specs=wide,
        out_shape=jax.ShapeDtypeStruct((rows, 2 * width), BF),
    )(near, *got, gate_up)


def gather_rows(v, n_y):
    first = permute_y(v, -1, n_y)
    far = permute_y(first, -1, n_y)
    last = permute_y(v, 1, n_y)
    return [v, first, far, last]


def relative(slab, half, y, n_y):
    rows = slab.shape[0] // (2 * n_y)
    return jnp.concatenate(
        [
            lax.dynamic_slice_in_dim(slab, (half * n_y + (y + (2 * half - 1) * d) % n_y) * rows, rows, 0)
            for d in range(n_y)
        ],
        axis=0,
    )


def absolute(part, y, core, n_y):
    rows = part.shape[0] // n_y
    return jnp.concatenate(
        [lax.dynamic_slice_in_dim(part, (((2 * core - 1) * (yy - y)) % n_y) * rows, rows, 0) for yy in range(n_y)],
        axis=0,
    )


def both_halves(own, other, core):
    flat = jnp.where(core == 0, jnp.stack([own, other]), jnp.stack([other, own]))
    return flat.reshape(2 * own.shape[0], own.shape[1])


def body(tokens, expert_ids, scores, weight_in, weight_out, out_grad):
    n_data = lax.axis_size("dp")
    n_y = lax.axis_size("expert") // 2
    here = lax.axis_index("expert")
    y, core = lax.div(here, 2), lax.rem(here, 2)
    tok_count, width = tokens.shape
    top_count = expert_ids.shape[1]
    capacity = min(tok_count, 5 * tok_count * top_count // (4 * n_data))
    slots = n_data * capacity

    ids_t = expert_ids.T
    scores_t = scores.T
    named = ids_t[:, None, :] == jnp.arange(n_data, dtype=jnp.int32)[None, :, None]
    hot = jnp.sum(named.astype(F32), axis=0)
    before = (
        jnp.arange(tok_count, dtype=jnp.int32)[:, None] < jnp.arange(tok_count, dtype=jnp.int32)[None, :]
    ).astype(BF)
    rank = dot(hot.astype(BF), before)
    position = jnp.where(hot > 0.0, rank, -1.0).astype(jnp.int32)
    placed = position[:, None, :] == jnp.arange(capacity, dtype=jnp.int32)[None, :, None]
    place = placed.astype(BF).reshape(slots, tok_count)

    token_send = dot(place, tokens).astype(BF)

    def exchange(v):
        v = v.reshape(n_data, capacity, width)
        return lax.all_to_all(v, "dp", split_axis=0, concat_axis=0, tiled=True).reshape(slots, width)

    in_own, out_own = weight_in[0], weight_out[0]
    token_slab = exchange(token_send)
    in_part = permute_core(in_own, n_y)
    out_part = permute_core(out_own, n_y)

    places = lax.rem(y + n_y + (2 * core - 1) * jnp.arange(n_y, dtype=jnp.int32), n_y)
    order = core * n_y + places
    scores_t, places, order, _ = lax.optimization_barrier((scores_t, places, order, token_send))
    score_total = jnp.sum(scores_t, axis=0, keepdims=True)
    weights_t = ROUTE_SCALE * scores_t / score_total
    weight_of = jnp.sum(jnp.where(named, weights_t[:, None, :], 0.0), axis=0)
    weight_place = jnp.where(placed, weight_of[:, None, :], 0.0).reshape(slots, tok_count)
    row_weight = jnp.sum(weight_place, axis=1, keepdims=True)
    grad_rows = dot(place, out_grad)
    grad_send = (row_weight * grad_rows).astype(BF)
    grad_send, grad_rows = lax.optimization_barrier((grad_send, grad_rows.astype(BF)))
    grad_slab = exchange(grad_send)

    token_slab, _ = lax.optimization_barrier((token_slab, grad_send[:8]))
    tok_part = permute_core(relative(token_slab, 1 - core, y, n_y), n_y)
    near, *far = partial_halves(token_slab, tok_part, in_own, in_part, order)
    up_2 = permute_y(far[2], 1, n_y)
    dn_2 = permute_y(far[3], -1, n_y)
    up_b = permute_y(far[1], 1, n_y)
    dn_a = permute_y(far[4], -1, n_y)
    up_1 = (far[0] + up_2.astype(F32)).astype(BF)
    dn_3 = (far[5] + dn_2.astype(F32)).astype(BF)
    up_a = permute_y(up_1, 1, n_y)
    dn_b = permute_y(dn_3, -1, n_y)
    got = [up_a, dn_a, up_b, dn_b]
    gate_up, hidden = hidden_rows(near, got)
    hidden = hidden.astype(BF)
    hid_parts = [permute_y(hidden, -d, n_y) for d in range(1, n_y)]

    grad_slab, _ = lax.optimization_barrier((grad_slab, up_1))
    grad_part = permute_core(relative(grad_slab, 1 - core, y, n_y), n_y)
    near, *far = partial_products(grad_slab, grad_part, out_own, out_part, order, True)
    got = send_far(far, n_y)
    gate_up_grad = gate_grad(near, got, gate_up)
    grad_slab, _ = lax.optimization_barrier((grad_slab, gate_up_grad))
    grad_own = relative(grad_slab, core, y, n_y)
    token_slab, _ = lax.optimization_barrier((token_slab, gate_up_grad))
    tok_own = relative(token_slab, core, y, n_y)

    hid = jnp.concatenate([hidden] + hid_parts, axis=0)
    out_other = permute_core(absolute(dot(hid, out_part).astype(BF), y, core, n_y), n_y)
    out_mine = absolute(dot(hid, out_own).astype(BF), y, core, n_y)
    expert_out = both_halves(out_mine, out_other, core)
    out_back = exchange(expert_out)

    gug = jnp.concatenate(gather_rows(gate_up_grad, n_y), axis=0)
    other_rows = absolute(dot_t(gug, in_part).astype(BF), y, core, n_y)
    grad_other = permute_core(other_rows, n_y)
    in_late, _ = lax.optimization_barrier((in_own, other_rows))
    grad_mine = absolute(dot_t(gug, in_late).astype(BF), y, core, n_y)
    choice_grad = both_halves(grad_mine, grad_other, core)
    grad_back = exchange(choice_grad)

    tok_part, tok_own, _ = lax.optimization_barrier((tok_part, tok_own, choice_grad))
    w_out_other = permute_core(gather_dot(hid, grad_part), n_y)
    w_out_grad = (gather_dot(hid, grad_own) + w_out_other).astype(BF)
    w_in_other = permute_core(gather_dot(tok_part, gug), n_y)
    w_in_grad = (gather_dot(tok_own, gug) + w_in_other).astype(BF)

    high = lax.reduce_precision(weight_place, 8, 7)
    low = (weight_place - high).astype(BF)
    high = high.astype(BF)
    layer_out = (gather_dot(high, out_back) + gather_dot(low, out_back)).astype(BF)
    slot_dot = jnp.sum(grad_rows.astype(F32) * out_back.astype(F32), axis=1)
    slot_dot = slot_dot.reshape(n_data, capacity)
    bit = 1
    while bit < 2 * n_y:
        slot_dot = slot_dot + permute_xor(slot_dot, bit, n_y)
        bit = 2 * bit
    dot_of = jnp.sum(jnp.where(placed, slot_dot[:, :, None], 0.0), axis=1)
    choice_dot = jnp.sum(jnp.where(named, dot_of[None, :, :], 0.0), axis=1)
    scores_grad = (
        ROUTE_SCALE * choice_dot - jnp.sum(choice_dot * weights_t, axis=0, keepdims=True)
    ) / score_total
    tokens_grad = gather_dot(place, grad_back).astype(BF)
    return layer_out, tokens_grad, scores_grad.T, w_in_grad[None], w_out_grad[None]


def solution(mesh):
    return jax.shard_map(
        body,
        mesh=mesh,
        in_specs=(
            P("dp", "expert"),
            P("dp", None),
            P("dp", None),
            P("dp", "expert", None),
            P("dp", None, "expert"),
            P("dp", "expert"),
        ),
        out_specs=(
            P("dp", "expert"),
            P("dp", "expert"),
            P("dp", None),
            P("dp", "expert", None),
            P("dp", None, "expert"),
        ),
        check_vma=False,
    )
```

```python
import functools

import jax
import jax.numpy as jnp
from jax import lax
from jax.experimental import pallas as pl
from jax.experimental.pallas import tpu as pltpu
from jax.sharding import PartitionSpec as P


ROUTE_SCALE = 2.5
BF = jnp.bfloat16
F32 = jnp.float32


def permute_y(v, step, n_y):
    return lax.ppermute(
        v,
        "expert",
        [(2 * y + c, 2 * ((y + (2 * c - 1) * step) % n_y) + c) for y in range(n_y) for c in range(2)],
    )


def permute_core(v, n_y):
    return lax.ppermute(
        v, "expert", [(2 * y + c, 2 * y + 1 - c) for y in range(n_y) for c in range(2)]
    )


def dot(a, b):
    return jnp.dot(a, b, preferred_element_type=F32)


def dot_t(a, b):
    return jnp.einsum("rd,fd->rf", a, b, preferred_element_type=F32)


def gather_dot(a, b):
    return jnp.einsum("rd,rf->df", a, b, preferred_element_type=F32)


def permute_xor(v, bit, n_y):
    return lax.ppermute(v, "expert", [(e, e ^ bit) for e in range(2 * n_y)])


def partial_kernel(order, own0, own1, own2, own3, part, w_own, w_part, near, *far, turned):
    rows = near.shape[0]
    contract = (((1,), (1 if turned else 0,)), ((), ()))
    own = jnp.concatenate([own0[...], own1[...], own2[...], own3[...]], axis=0)
    total = lax.dot_general(own, w_own[...], contract, preferred_element_type=F32)
    total = total + lax.dot_general(part[...], w_part[...], contract, preferred_element_type=F32)
    near[...] = total[:rows]
    for k, out in enumerate(far):
        out[...] = total[(k + 1) * rows : (k + 2) * rows].astype(BF)


def partial_products(slab, part, w_own, w_part, order, turned):
    n_y = order.shape[0]
    rows = part.shape[0] // n_y
    k = slab.shape[1]
    width = w_own.shape[0] if turned else w_own.shape[1]
    chunk = width // 4

    def rows_of(d):
        return pl.BlockSpec((rows, k), lambda j, order: (order[d], 0))

    if turned:
        weight = pl.BlockSpec((chunk, k), lambda j, order: (j, 0))
    else:
        weight = pl.BlockSpec((k, chunk), lambda j, order: (0, j))
    out = pl.BlockSpec((rows, chunk), lambda j, order: (0, j))
    return pl.pallas_call(
        functools.partial(partial_kernel, turned=turned),
        compiler_params=pltpu.CompilerParams(vmem_limit_bytes=24 * 1024 * 1024),
        grid_spec=pltpu.PrefetchScalarGridSpec(
            num_scalar_prefetch=1,
            grid=(width // chunk,),
            in_specs=[rows_of(d) for d in range(4)]
            + [pl.BlockSpec(part.shape, lambda j, order: (0, 0)), weight, weight],
            out_specs=[out, out, out, out],
        ),
        out_shape=[jax.ShapeDtypeStruct((rows, width), F32)]
        + [jax.ShapeDtypeStruct((rows, width), BF)] * 3,
    )(order, slab, slab, slab, slab, part, w_own, w_part)


def halves_kernel(order, own0, own1, own2, own3, part, w_own, w_part, near, *far):
    rows = near.shape[0]
    half = rows // 2
    own = jnp.concatenate([own0[...], own1[...], own2[...], own3[...]], axis=0)
    total = jnp.dot(own, w_own[...], preferred_element_type=F32)
    total = total + jnp.dot(part[...], w_part[...], preferred_element_type=F32)
    near[...] = total[:rows]
    for k, out in enumerate(far):
        out[...] = total[rows + k * half : rows + (k + 1) * half].astype(out.dtype)


def partial_halves(slab, part, w_own, w_part, order):
    n_y = order.shape[0]
    rows = part.shape[0] // n_y
    k = slab.shape[1]
    width = w_own.shape[1]
    chunk = width // 4

    def rows_of(d):
        return pl.BlockSpec((rows, k), lambda j, order: (order[d], 0))

    weight = pl.BlockSpec((k, chunk), lambda j, order: (0, j))
    half = pl.BlockSpec((rows // 2, chunk), lambda j, order: (0, j))
    kinds = [F32, BF, BF, BF, BF, F32]
    return pl.pallas_call(
        halves_kernel,
        compiler_params=pltpu.CompilerParams(vmem_limit_bytes=24 * 1024 * 1024),
        grid_spec=pltpu.PrefetchScalarGridSpec(
            num_scalar_prefetch=1,
            grid=(width // chunk,),
            in_specs=[rows_of(d) for d in range(4)]
            + [pl.BlockSpec(part.shape, lambda j, order: (0, 0)), weight, weight],
            out_specs=[pl.BlockSpec((rows, chunk), lambda j, order: (0, j))] + [half] * 6,
        ),
        out_shape=[jax.ShapeDtypeStruct((rows, width), F32)]
        + [jax.ShapeDtypeStruct((rows // 2, width), kind) for kind in kinds],
    )(order, slab, slab, slab, slab, part, w_own, w_part)


def send_far(far, n_y):
    return [permute_y(piece, d + 1, n_y) for d, piece in enumerate(far)]


def hidden_kernel(near, up_a, dn_a, up_b, dn_b, gate_up, hidden):
    half, width = up_a.shape
    for k, (up, dn) in enumerate(((up_a, dn_a), (up_b, dn_b))):
        rows = pl.ds(k * half, half)
        total = near[rows, :] + up[...].astype(F32) + dn[...].astype(F32)
        gate_up[rows, :] = total
        gate, upward = total[:, : width // 2], total[:, width // 2 :]
        hidden[rows, :] = gate * jax.nn.sigmoid(gate) * upward


def hidden_rows(near, got):
    rows, width = near.shape
    return pl.pallas_call(
        hidden_kernel,
        compiler_params=pltpu.CompilerParams(vmem_limit_bytes=24 * 1024 * 1024),
        out_shape=[
            jax.ShapeDtypeStruct((rows, width), F32),
            jax.ShapeDtypeStruct((rows, width // 2), F32),
        ],
    )(near, *got)


def gate_grad_kernel(near, first, second, third, gate_up, out):
    width = near.shape[1]
    grad = near[...] + first[...].astype(F32) + second[...].astype(F32) + third[...].astype(F32)
    gate, up = gate_up[:, :width], gate_up[:, width:]
    sig = jax.nn.sigmoid(gate)
    out[:, :width] = (grad * up * sig * (1.0 + gate * (1.0 - sig))).astype(BF)
    out[:, width:] = (grad * gate * sig).astype(BF)


def gate_grad(near, got, gate_up):
    rows, width = near.shape
    tile = rows // 2
    narrow = pl.BlockSpec((tile, width), lambda i: (i, 0))
    wide = pl.BlockSpec((tile, 2 * width), lambda i: (i, 0))
    return pl.pallas_call(
        gate_grad_kernel,
        compiler_params=pltpu.CompilerParams(vmem_limit_bytes=24 * 1024 * 1024),
        grid=(2,),
        in_specs=[narrow, narrow, narrow, narrow, wide],
        out_specs=wide,
        out_shape=jax.ShapeDtypeStruct((rows, 2 * width), BF),
    )(near, *got, gate_up)


def gather_rows(v, n_y):
    first = permute_y(v, -1, n_y)
    far = permute_y(first, -1, n_y)
    last = permute_y(v, 1, n_y)
    return [v, first, far, last]


def relative(slab, half, y, n_y):
    rows = slab.shape[0] // (2 * n_y)
    return jnp.concatenate(
        [
            lax.dynamic_slice_in_dim(slab, (half * n_y + (y + (2 * half - 1) * d) % n_y) * rows, rows, 0)
            for d in range(n_y)
        ],
        axis=0,
    )


def absolute(part, y, core, n_y):
    rows = part.shape[0] // n_y
    return jnp.concatenate(
        [lax.dynamic_slice_in_dim(part, (((2 * core - 1) * (yy - y)) % n_y) * rows, rows, 0) for yy in range(n_y)],
        axis=0,
    )


def both_halves(own, other, core):
    flat = jnp.where(core == 0, jnp.stack([own, other]), jnp.stack([other, own]))
    return flat.reshape(2 * own.shape[0], own.shape[1])


def body(tokens, expert_ids, scores, weight_in, weight_out, out_grad):
    n_data = lax.axis_size("dp")
    n_y = lax.axis_size("expert") // 2
    here = lax.axis_index("expert")
    y, core = lax.div(here, 2), lax.rem(here, 2)
    tok_count, width = tokens.shape
    top_count = expert_ids.shape[1]
    capacity = min(tok_count, 5 * tok_count * top_count // (4 * n_data))
    slots = n_data * capacity

    ids_t = expert_ids.T
    scores_t = scores.T
    named = ids_t[:, None, :] == jnp.arange(n_data, dtype=jnp.int32)[None, :, None]
    hot = jnp.sum(named.astype(F32), axis=0)
    before = (
        jnp.arange(tok_count, dtype=jnp.int32)[:, None] < jnp.arange(tok_count, dtype=jnp.int32)[None, :]
    ).astype(BF)
    rank = dot(hot.astype(BF), before)
    position = jnp.where(hot > 0.0, rank, -1.0).astype(jnp.int32)
    placed = position[:, None, :] == jnp.arange(capacity, dtype=jnp.int32)[None, :, None]
    place = placed.astype(BF).reshape(slots, tok_count)

    token_send = dot(place, tokens).astype(BF)

    def exchange(v):
        v = v.reshape(n_data, capacity, width)
        return lax.all_to_all(v, "dp", split_axis=0, concat_axis=0, tiled=True).reshape(slots, width)

    in_own, out_own = weight_in[0], weight_out[0]
    token_slab = exchange(token_send)
    in_part = permute_core(in_own, n_y)
    out_part = permute_core(out_own, n_y)

    places = lax.rem(y + n_y + (2 * core - 1) * jnp.arange(n_y, dtype=jnp.int32), n_y)
    order = core * n_y + places
    scores_t, places, order, _ = lax.optimization_barrier((scores_t, places, order, token_send))
    score_total = jnp.sum(scores_t, axis=0, keepdims=True)
    weights_t = ROUTE_SCALE * scores_t / score_total
    weight_of = jnp.sum(jnp.where(named, weights_t[:, None, :], 0.0), axis=0)
    weight_place = jnp.where(placed, weight_of[:, None, :], 0.0).reshape(slots, tok_count)
    row_weight = jnp.sum(weight_place, axis=1, keepdims=True)
    grad_rows = dot(place, out_grad)
    grad_send = (row_weight * grad_rows).astype(BF)
    grad_send, grad_rows = lax.optimization_barrier((grad_send, grad_rows.astype(BF)))
    grad_slab = exchange(grad_send)

    token_slab, _ = lax.optimization_barrier((token_slab, grad_send[:8]))
    tok_part = permute_core(relative(token_slab, 1 - core, y, n_y), n_y)
    near, *far = partial_halves(token_slab, tok_part, in_own, in_part, order)
    up_2 = permute_y(far[2], 1, n_y)
    dn_2 = permute_y(far[3], -1, n_y)
    up_b = permute_y(far[1], 1, n_y)
    dn_a = permute_y(far[4], -1, n_y)
    up_1 = (far[0] + up_2.astype(F32)).astype(BF)
    dn_3 = (far[5] + dn_2.astype(F32)).astype(BF)
    up_a = permute_y(up_1, 1, n_y)
    dn_b = permute_y(dn_3, -1, n_y)
    got = [up_a, dn_a, up_b, dn_b]
    gate_up, hidden = hidden_rows(near, got)
    hidden = hidden.astype(BF)
    hid_parts = [permute_y(hidden, -d, n_y) for d in range(1, n_y)]

    grad_slab, _ = lax.optimization_barrier((grad_slab, up_1))
    grad_part = permute_core(relative(grad_slab, 1 - core, y, n_y), n_y)
    near, *far = partial_products(grad_slab, grad_part, out_own, out_part, order, True)
    got = send_far(far, n_y)
    gate_up_grad = gate_grad(near, got, gate_up)
    grad_slab, _ = lax.optimization_barrier((grad_slab, gate_up_grad))
    grad_own = relative(grad_slab, core, y, n_y)
    token_slab, _ = lax.optimization_barrier((token_slab, gate_up_grad))
    tok_own = relative(token_slab, core, y, n_y)

    hid = jnp.concatenate([hidden] + hid_parts, axis=0)
    out_other = permute_core(absolute(dot(hid, out_part).astype(BF), y, core, n_y), n_y)
    out_mine = absolute(dot(hid, out_own).astype(BF), y, core, n_y)
    expert_out = both_halves(out_mine, out_other, core)
    out_back = exchange(expert_out)

    gug = jnp.concatenate(gather_rows(gate_up_grad, n_y), axis=0)
    other_rows = absolute(dot_t(gug, in_part).astype(BF), y, core, n_y)
    grad_other = permute_core(other_rows, n_y)
    y_late, _ = lax.optimization_barrier((y, other_rows))
    grad_mine = absolute(dot_t(gug, in_own).astype(BF), y_late, core, n_y)
    choice_grad = both_halves(grad_mine, grad_other, core)
    grad_back = exchange(choice_grad)

    tok_part, tok_own, _ = lax.optimization_barrier((tok_part, tok_own, choice_grad))
    w_out_other = permute_core(gather_dot(hid, grad_part), n_y)
    w_out_grad = (gather_dot(hid, grad_own) + w_out_other).astype(BF)
    w_in_other = permute_core(gather_dot(tok_part, gug), n_y)
    w_in_grad = (gather_dot(tok_own, gug) + w_in_other).astype(BF)

    high = lax.reduce_precision(weight_place, 8, 7)
    low = (weight_place - high).astype(BF)
    high = high.astype(BF)
    layer_out = (gather_dot(high, out_back) + gather_dot(low, out_back)).astype(BF)
    slot_dot = jnp.sum(grad_rows.astype(F32) * out_back.astype(F32), axis=1)
    slot_dot = slot_dot.reshape(n_data, capacity)
    bit = 1
    while bit < 2 * n_y:
        slot_dot = slot_dot + permute_xor(slot_dot, bit, n_y)
        bit = 2 * bit
    dot_of = jnp.sum(jnp.where(placed, slot_dot[:, :, None], 0.0), axis=1)
    choice_dot = jnp.sum(jnp.where(named, dot_of[None, :, :], 0.0), axis=1)
    scores_grad = (
        ROUTE_SCALE * choice_dot - jnp.sum(choice_dot * weights_t, axis=0, keepdims=True)
    ) / score_total
    tokens_grad = gather_dot(place, grad_back).astype(BF)
    return layer_out, tokens_grad, scores_grad.T, w_in_grad[None], w_out_grad[None]


def solution(mesh):
    return jax.shard_map(
        body,
        mesh=mesh,
        in_specs=(
            P("dp", "expert"),
            P("dp", None),
            P("dp", None),
            P("dp", "expert", None),
            P("dp", None, "expert"),
            P("dp", "expert"),
        ),
        out_specs=(
            P("dp", "expert"),
            P("dp", "expert"),
            P("dp", None),
            P("dp", "expert", None),
            P("dp", None, "expert"),
        ),
        check_vma=False,
    )
```

```python
import functools

import jax
import jax.numpy as jnp
from jax import lax
from jax.experimental import pallas as pl
from jax.experimental.pallas import tpu as pltpu
from jax.sharding import PartitionSpec as P


ROUTE_SCALE = 2.5
BF = jnp.bfloat16
F32 = jnp.float32


def permute_y(v, step, n_y):
    return lax.ppermute(
        v, "expert", [(2 * y + c, 2 * ((y + step) % n_y) + c) for y in range(n_y) for c in range(2)]
    )


def permute_core(v, n_y):
    return lax.ppermute(
        v, "expert", [(2 * y + c, 2 * y + 1 - c) for y in range(n_y) for c in range(2)]
    )


def dot(a, b):
    return jnp.dot(a, b, preferred_element_type=F32)


def dot_t(a, b):
    return jnp.einsum("rd,fd->rf", a, b, preferred_element_type=F32)


def gather_dot(a, b):
    return jnp.einsum("rd,rf->df", a, b, preferred_element_type=F32)


def permute_xor(v, bit, n_y):
    return lax.ppermute(v, "expert", [(e, e ^ bit) for e in range(2 * n_y)])


def partial_kernel(order, own0, own1, own2, own3, part, w_own, w_part, near, *far, turned):
    rows = near.shape[0]
    contract = (((1,), (1 if turned else 0,)), ((), ()))
    own = jnp.concatenate([own0[...], own1[...], own2[...], own3[...]], axis=0)
    total = lax.dot_general(own, w_own[...], contract, preferred_element_type=F32)
    total = total + lax.dot_general(part[...], w_part[...], contract, preferred_element_type=F32)
    near[...] = total[:rows]
    for k, out in enumerate(far):
        out[...] = total[(k + 1) * rows : (k + 2) * rows].astype(BF)


def partial_products(slab, part, w_own, w_part, order, turned):
    n_y = order.shape[0]
    rows = part.shape[0] // n_y
    k = slab.shape[1]
    width = w_own.shape[0] if turned else w_own.shape[1]
    chunk = width // 4

    def rows_of(d):
        return pl.BlockSpec((rows, k), lambda j, order: (order[d], 0))

    if turned:
        weight = pl.BlockSpec((chunk, k), lambda j, order: (j, 0))
    else:
        weight = pl.BlockSpec((k, chunk), lambda j, order: (0, j))
    out = pl.BlockSpec((rows, chunk), lambda j, order: (0, j))
    return pl.pallas_call(
        functools.partial(partial_kernel, turned=turned),
        compiler_params=pltpu.CompilerParams(vmem_limit_bytes=24 * 1024 * 1024),
        grid_spec=pltpu.PrefetchScalarGridSpec(
            num_scalar_prefetch=1,
            grid=(width // chunk,),
            in_specs=[rows_of(d) for d in range(4)]
            + [pl.BlockSpec(part.shape, lambda j, order: (0, 0)), weight, weight],
            out_specs=[out, out, out, out],
        ),
        out_shape=[jax.ShapeDtypeStruct((rows, width), F32)]
        + [jax.ShapeDtypeStruct((rows, width), BF)] * 3,
    )(order, slab, slab, slab, slab, part, w_own, w_part)


def halves_kernel(order, own0, own1, own2, own3, part, w_own, w_part, near, *far):
    rows = near.shape[0]
    half = rows // 2
    own = jnp.concatenate([own0[...], own1[...], own2[...], own3[...]], axis=0)
    total = jnp.dot(own, w_own[...], preferred_element_type=F32)
    total = total + jnp.dot(part[...], w_part[...], preferred_element_type=F32)
    near[...] = total[:rows]
    for k, out in enumerate(far):
        out[...] = total[rows + k * half : rows + (k + 1) * half].astype(out.dtype)


def partial_halves(slab, part, w_own, w_part, order):
    n_y = order.shape[0]
    rows = part.shape[0] // n_y
    k = slab.shape[1]
    width = w_own.shape[1]
    chunk = width // 4

    def rows_of(d):
        return pl.BlockSpec((rows, k), lambda j, order: (order[d], 0))

    weight = pl.BlockSpec((k, chunk), lambda j, order: (0, j))
    half = pl.BlockSpec((rows // 2, chunk), lambda j, order: (0, j))
    kinds = [F32, BF, BF, BF, BF, F32]
    return pl.pallas_call(
        halves_kernel,
        compiler_params=pltpu.CompilerParams(vmem_limit_bytes=24 * 1024 * 1024),
        grid_spec=pltpu.PrefetchScalarGridSpec(
            num_scalar_prefetch=1,
            grid=(width // chunk,),
            in_specs=[rows_of(d) for d in range(4)]
            + [pl.BlockSpec(part.shape, lambda j, order: (0, 0)), weight, weight],
            out_specs=[pl.BlockSpec((rows, chunk), lambda j, order: (0, j))] + [half] * 6,
        ),
        out_shape=[jax.ShapeDtypeStruct((rows, width), F32)]
        + [jax.ShapeDtypeStruct((rows // 2, width), kind) for kind in kinds],
    )(order, slab, slab, slab, slab, part, w_own, w_part)


def send_far(far, n_y):
    return [permute_y(piece, d + 1, n_y) for d, piece in enumerate(far)]


def hidden_kernel(near, up_a, dn_a, up_b, dn_b, gate_up, hidden):
    half, width = up_a.shape
    for k, (up, dn) in enumerate(((up_a, dn_a), (up_b, dn_b))):
        rows = pl.ds(k * half, half)
        total = near[rows, :] + up[...].astype(F32) + dn[...].astype(F32)
        gate_up[rows, :] = total
        gate, upward = total[:, : width // 2], total[:, width // 2 :]
        hidden[rows, :] = gate * jax.nn.sigmoid(gate) * upward


def hidden_rows(near, got):
    rows, width = near.shape
    return pl.pallas_call(
        hidden_kernel,
        compiler_params=pltpu.CompilerParams(vmem_limit_bytes=24 * 1024 * 1024),
        out_shape=[
            jax.ShapeDtypeStruct((rows, width), F32),
            jax.ShapeDtypeStruct((rows, width // 2), F32),
        ],
    )(near, *got)


def gate_grad_kernel(near, first, second, third, gate_up, out):
    width = near.shape[1]
    grad = near[...] + first[...].astype(F32) + second[...].astype(F32) + third[...].astype(F32)
    gate, up = gate_up[:, :width], gate_up[:, width:]
    sig = jax.nn.sigmoid(gate)
    out[:, :width] = (grad * up * sig * (1.0 + gate * (1.0 - sig))).astype(BF)
    out[:, width:] = (grad * gate * sig).astype(BF)


def gate_grad(near, got, gate_up):
    rows, width = near.shape
    tile = rows // 2
    narrow = pl.BlockSpec((tile, width), lambda i: (i, 0))
    wide = pl.BlockSpec((tile, 2 * width), lambda i: (i, 0))
    return pl.pallas_call(
        gate_grad_kernel,
        compiler_params=pltpu.CompilerParams(vmem_limit_bytes=24 * 1024 * 1024),
        grid=(2,),
        in_specs=[narrow, narrow, narrow, narrow, wide],
        out_specs=wide,
        out_shape=jax.ShapeDtypeStruct((rows, 2 * width), BF),
    )(near, *got, gate_up)


def permute_by_core(v, n_y):
    return lax.ppermute(
        v,
        "expert",
        [(2 * y + c, 2 * ((y + 1 - 2 * c) % n_y) + c) for y in range(n_y) for c in range(2)],
    )


def gather_rows(v, core, n_y):
    dn = permute_y(v, 1, n_y)
    up = permute_y(v, -1, n_y)
    far = permute_by_core(jnp.where(core == 0, dn, up), n_y)
    return [v, up, far, dn]


def relative(slab, half, y, n_y):
    rows = slab.shape[0] // (2 * n_y)
    return jnp.concatenate(
        [
            lax.dynamic_slice_in_dim(slab, (half * n_y + (y + d) % n_y) * rows, rows, 0)
            for d in range(n_y)
        ],
        axis=0,
    )


def absolute(part, y, n_y):
    rows = part.shape[0] // n_y
    return jnp.concatenate(
        [lax.dynamic_slice_in_dim(part, ((yy - y) % n_y) * rows, rows, 0) for yy in range(n_y)],
        axis=0,
    )


def both_halves(own, other, core):
    flat = jnp.where(core == 0, jnp.stack([own, other]), jnp.stack([other, own]))
    return flat.reshape(2 * own.shape[0], own.shape[1])


def body(tokens, expert_ids, scores, weight_in, weight_out, out_grad):
    n_data = lax.axis_size("dp")
    n_y = lax.axis_size("expert") // 2
    here = lax.axis_index("expert")
    y, core = lax.div(here, 2), lax.rem(here, 2)
    tok_count, width = tokens.shape
    top_count = expert_ids.shape[1]
    capacity = min(tok_count, 5 * tok_count * top_count // (4 * n_data))
    slots = n_data * capacity

    ids_t = expert_ids.T
    scores_t = scores.T
    named = ids_t[:, None, :] == jnp.arange(n_data, dtype=jnp.int32)[None, :, None]
    hot = jnp.sum(named.astype(F32), axis=0)
    before = (
        jnp.arange(tok_count, dtype=jnp.int32)[:, None] < jnp.arange(tok_count, dtype=jnp.int32)[None, :]
    ).astype(BF)
    rank = dot(hot.astype(BF), before)
    position = jnp.where(hot > 0.0, rank, -1.0).astype(jnp.int32)
    placed = position[:, None, :] == jnp.arange(capacity, dtype=jnp.int32)[None, :, None]
    place = placed.astype(BF).reshape(slots, tok_count)

    token_send = dot(place, tokens).astype(BF)

    def exchange(v):
        v = v.reshape(n_data, capacity, width)
        return lax.all_to_all(v, "dp", split_axis=0, concat_axis=0, tiled=True).reshape(slots, width)

    in_own, out_own = weight_in[0], weight_out[0]
    token_slab = exchange(token_send)
    in_part = permute_core(in_own, n_y)
    out_part = permute_core(out_own, n_y)

    places = lax.rem(y + jnp.arange(n_y, dtype=jnp.int32), n_y)
    order = core * n_y + places
    scores_t, places, order, _ = lax.optimization_barrier((scores_t, places, order, token_send))
    score_total = jnp.sum(scores_t, axis=0, keepdims=True)
    weights_t = ROUTE_SCALE * scores_t / score_total
    weight_of = jnp.sum(jnp.where(named, weights_t[:, None, :], 0.0), axis=0)
    weight_place = jnp.where(placed, weight_of[:, None, :], 0.0).reshape(slots, tok_count)
    row_weight = jnp.sum(weight_place, axis=1, keepdims=True)
    grad_rows = dot(place, out_grad)
    grad_send = (row_weight * grad_rows).astype(BF)
    grad_send, grad_rows = lax.optimization_barrier((grad_send, grad_rows.astype(BF)))
    grad_slab = exchange(grad_send)

    token_slab, _ = lax.optimization_barrier((token_slab, grad_send[:8]))
    tok_part = permute_core(relative(token_slab, 1 - core, y, n_y), n_y)
    near, *far = partial_halves(token_slab, tok_part, in_own, in_part, order)
    up_2 = permute_y(far[2], 1, n_y)
    dn_2 = permute_y(far[3], -1, n_y)
    up_b = permute_y(far[1], 1, n_y)
    dn_a = permute_y(far[4], -1, n_y)
    up_1 = (far[0] + up_2.astype(F32)).astype(BF)
    dn_3 = (far[5] + dn_2.astype(F32)).astype(BF)
    up_a = permute_y(up_1, 1, n_y)
    dn_b = permute_y(dn_3, -1, n_y)
    got = [up_a, dn_a, up_b, dn_b]
    gate_up, hidden = hidden_rows(near, got)
    hidden = hidden.astype(BF)
    hid_parts = [permute_y(hidden, -d, n_y) for d in range(1, n_y)]

    grad_slab, _ = lax.optimization_barrier((grad_slab, up_1))
    grad_part = permute_core(relative(grad_slab, 1 - core, y, n_y), n_y)
    near, *far = partial_products(grad_slab, grad_part, out_own, out_part, order, True)
    got = send_far(far, n_y)
    gate_up_grad = gate_grad(near, got, gate_up)
    grad_slab, _ = lax.optimization_barrier((grad_slab, gate_up_grad))
    grad_own = relative(grad_slab, core, y, n_y)
    token_slab, _ = lax.optimization_barrier((token_slab, gate_up_grad))
    tok_own = relative(token_slab, core, y, n_y)

    hid = jnp.concatenate([hidden] + hid_parts, axis=0)
    out_other = permute_core(absolute(dot(hid, out_part).astype(BF), y, n_y), n_y)
    out_mine = absolute(dot(hid, out_own).astype(BF), y, n_y)
    expert_out = both_halves(out_mine, out_other, core)
    out_back = exchange(expert_out)

    gug = jnp.concatenate(gather_rows(gate_up_grad, core, n_y), axis=0)
    grad_other = permute_core(absolute(dot_t(gug, in_part).astype(BF), y, n_y), n_y)
    grad_mine = absolute(dot_t(gug, in_own).astype(BF), y, n_y)
    choice_grad = both_halves(grad_mine, grad_other, core)
    grad_back = exchange(choice_grad)

    tok_part, tok_own, _ = lax.optimization_barrier((tok_part, tok_own, choice_grad))
    w_out_other = permute_core(gather_dot(hid, grad_part), n_y)
    w_out_grad = (gather_dot(hid, grad_own) + w_out_other).astype(BF)
    w_in_other = permute_core(gather_dot(tok_part, gug), n_y)
    w_in_grad = (gather_dot(tok_own, gug) + w_in_other).astype(BF)

    high = lax.reduce_precision(weight_place, 8, 7)
    low = (weight_place - high).astype(BF)
    high = high.astype(BF)
    layer_out = (gather_dot(high, out_back) + gather_dot(low, out_back)).astype(BF)
    slot_dot = jnp.sum(grad_rows.astype(F32) * out_back.astype(F32), axis=1)
    slot_dot = slot_dot.reshape(n_data, capacity)
    bit = 1
    while bit < 2 * n_y:
        slot_dot = slot_dot + permute_xor(slot_dot, bit, n_y)
        bit = 2 * bit
    dot_of = jnp.sum(jnp.where(placed, slot_dot[:, :, None], 0.0), axis=1)
    choice_dot = jnp.sum(jnp.where(named, dot_of[None, :, :], 0.0), axis=1)
    scores_grad = (
        ROUTE_SCALE * choice_dot - jnp.sum(choice_dot * weights_t, axis=0, keepdims=True)
    ) / score_total
    tokens_grad = gather_dot(place, grad_back).astype(BF)
    return layer_out, tokens_grad, scores_grad.T, w_in_grad[None], w_out_grad[None]


def solution(mesh):
    return jax.shard_map(
        body,
        mesh=mesh,
        in_specs=(
            P("dp", "expert"),
            P("dp", None),
            P("dp", None),
            P("dp", "expert", None),
            P("dp", None, "expert"),
            P("dp", "expert"),
        ),
        out_specs=(
            P("dp", "expert"),
            P("dp", "expert"),
            P("dp", None),
            P("dp", "expert", None),
            P("dp", None, "expert"),
        ),
        check_vma=False,
    )
```
